256 devices in a mesh: section: 16 (over x, y), ctx: 16 (over z, core).
Axes of the slice: x: 4, y: 4, z: 8, core: 2. Of those that a mesh axis runs over, the one named last changes fastest.
Arguments:
- queries: bfloat16 [2, 16, 2048, 1024], P(None, 'section', 'ctx'), may hold values from -8 to 8
- out_grad: bfloat16 [2, 16, 2048, 1024], P(None, 'section', 'ctx'), may hold values from -6 to 6
- keys: bfloat16 [16, 2048, 128], P('section', 'ctx'), may hold values from -4 to 4
- values: bfloat16 [16, 2048, 128], P('section', 'ctx'), may hold values from -6 to 6
- entering_keys: bfloat16 [2048, 128], P('ctx'), may hold values from -4 to 4
- entering_values: bfloat16 [2048, 128], P('ctx'), may hold values from -6 to 6
- key_grads_in: float32 [16, 2048, 128], P('section', 'ctx'), may hold values from -4 to 4
- value_grads_in: float32 [16, 2048, 128], P('section', 'ctx'), may hold values from -4 to 4
- group_order: int32 [16], replicated, may hold values from 0 to 15, each once
Outputs:
- query_grads: bfloat16 [2, 16, 2048, 1024], P(None, 'section', 'ctx')
- key_grads: float32 [2, 16, 2048, 128], P(None, 'section', 'ctx')
- value_grads: float32 [2, 16, 2048, 128], P(None, 'section', 'ctx')
The draws below stay inside these ranges and needn't reach their ends.
Inputs may be any that keep to these rules, and one draw needn't show every extreme that they name: `group_order`: each number 0 to 15 appears once.
All inputs are finite; a program needn't handle non-finite values.
Results may differ from the reference program's by a relative error of at most 0.0062.
Values may be sent and summed in bfloat16 or wider, within the bound.
A program may use at most 128 MiB of HBM per device.

```python
import jax
import jax.numpy as jnp
from jax import lax

CTX_DEV = 128
HEADS = 8
HEAD_DIM = 128
TICKS = 2
GROUPS = 16
SEQ = 2048
SECTIONS = 16


def key_tables(key):
    normal_part = jax.random.normal(jax.random.fold_in(key, 11), (SECTIONS + 1, SEQ, HEAD_DIM), jnp.float32)
    normal_part = jnp.clip(normal_part, -4.0, 4.0)
    return normal_part


def draw_keys(key, part):
    return key_tables(key)[:SECTIONS].astype(jnp.bfloat16)


def draw_entering_keys(key, part):
    return key_tables(key)[SECTIONS].astype(jnp.bfloat16)


def draw_queries(key, part):
    normal_part = jax.random.normal(jax.random.fold_in(key, 23), (TICKS, SECTIONS, SEQ, HEADS, HEAD_DIM), jnp.float32)
    normal_part = jnp.clip(normal_part, -4.0, 4.0)
    return normal_part.reshape(TICKS, SECTIONS, SEQ, HEADS * HEAD_DIM).astype(jnp.bfloat16)


def block_scale(rng, shape, split, low, top_value):
    def one(axis_at, shards_of):
        steps = jax.random.uniform(jax.random.fold_in(jax.random.fold_in(rng, 6), axis_at), (shards_of,), jnp.float32, low / len(split), top_value / len(split))
        return jnp.repeat(jnp.exp(steps), shape[axis_at] // shards_of).reshape((-1,) + (1,) * (len(shape) - axis_at - 1))

    level = one(*split[0])
    for cut in split[1:]:
        level = level * one(*cut)
    return level


def bell_draw(key, extent, deviation, bound, split=(), kind=jnp.bfloat16):
    loudness = block_scale(key, extent, split, -0.22, 0.18) if split else 1.0
    values = jax.random.normal(key, extent, jnp.float32) * deviation * loudness
    return jnp.minimum(jnp.maximum(values, -bound), bound).astype(kind)


def setup_inputs(seed: int = 0) -> dict:
    key_list = jax.random.split(jax.random.key(seed), 10)
    return {
        "queries": draw_queries(jax.random.fold_in(key_list[9], 71), 0),
        "out_grad": bell_draw(key_list[1], (TICKS, SECTIONS, SEQ, HEADS * HEAD_DIM), 1.0, 6.0, ((1, 16), (2, 16))),
        "keys": draw_keys(jax.random.fold_in(key_list[9], 71), 0),
        "values": bell_draw(key_list[3], (SECTIONS, SEQ, HEAD_DIM), 1.0, 6.0, ((0, 16), (1, 16))),
        "entering_keys": draw_entering_keys(jax.random.fold_in(key_list[9], 71), 0),
        "entering_values": bell_draw(key_list[5], (SEQ, HEAD_DIM), 1.0, 6.0, ((0, 16),)),
        "key_grads_in": bell_draw(key_list[6], (SECTIONS, SEQ, HEAD_DIM), 0.25, 4.0, ((0, 16), (1, 16)), jnp.float32),
        "value_grads_in": bell_draw(key_list[7], (SECTIONS, SEQ, HEAD_DIM), 0.25, 4.0, ((0, 16), (1, 16)), jnp.float32),
        "group_order": jax.random.permutation(key_list[8], GROUPS).astype(jnp.int32),
    }


MASK_FILL = -1e30


def token_positions(group_order):
    row_ids = jnp.arange(SEQ, dtype=jnp.int32)
    return (group_order[row_ids // CTX_DEV] * CTX_DEV + row_ids % CTX_DEV).astype(jnp.int32)


def attend_back(query_all, grad_all, key_block, value_block, positions):
    score_scale = 1.0 / (HEAD_DIM ** 0.5)
    query_heads = query_all.reshape(SEQ, HEADS, HEAD_DIM)
    grad_heads = grad_all.reshape(SEQ, HEADS, HEAD_DIM)
    allowed = positions[None, :] <= positions[:, None]
    query_parts = []
    key_total = jnp.zeros((SEQ, HEAD_DIM), jnp.float32)
    value_total = jnp.zeros((SEQ, HEAD_DIM), jnp.float32)
    for head in range(HEADS):
        scores = jnp.dot(query_heads[:, head], key_block.T, preferred_element_type=jnp.float32) * score_scale
        scores = jnp.where(allowed, scores, MASK_FILL)
        biggest = jnp.max(scores, axis=1, keepdims=True)
        expo = jnp.where(allowed, jnp.exp(scores - biggest), 0.0)
        probs = expo / jnp.sum(expo, axis=1, keepdims=True)
        prob_grads = jnp.dot(grad_heads[:, head], value_block.T, preferred_element_type=jnp.float32)
        deltas = jnp.sum(probs * prob_grads, axis=1, keepdims=True)
        score_grad = (probs * (prob_grads - deltas)).astype(jnp.bfloat16)
        probs_half = probs.astype(jnp.bfloat16)
        query_parts.append((jnp.dot(score_grad, key_block, preferred_element_type=jnp.float32) * score_scale).astype(jnp.bfloat16))
        key_total = key_total + jnp.dot(score_grad.T, query_heads[:, head], preferred_element_type=jnp.float32) * score_scale
        value_total = value_total + jnp.dot(probs_half.T, grad_heads[:, head], preferred_element_type=jnp.float32)
    return jnp.stack(query_parts, axis=1).reshape(SEQ, HEADS * HEAD_DIM), key_total, value_total


def reference(queries, out_grad, keys, values, entering_keys, entering_values, key_grads_in, value_grads_in, group_order):
    positions = token_positions(group_order)

    def section_step(operands):
        query_all, grad_all, key_block, value_block, key_acc, value_acc = operands
        query_grad, key_total, value_total = attend_back(query_all, grad_all, key_block, value_block, positions)
        return query_grad, key_acc + key_total, value_acc + value_total

    first = lax.map(section_step, (queries[0], out_grad[0], keys, values, key_grads_in, value_grads_in))
    next_keys = jnp.concatenate([keys[1:], entering_keys[None]], axis=0)
    next_values = jnp.concatenate([values[1:], entering_values[None]], axis=0)
    next_key_acc = jnp.concatenate([first[1][1:], jnp.zeros_like(first[1][:1])], axis=0)
    next_value_acc = jnp.concatenate([first[2][1:], jnp.zeros_like(first[2][:1])], axis=0)
    second = lax.map(section_step, (queries[1], out_grad[1], next_keys, next_values, next_key_acc, next_value_acc))
    query_grads = jnp.stack([first[0], second[0]], axis=0)
    key_grads = jnp.stack([first[1], second[1]], axis=0)
    value_grads = jnp.stack([first[2], second[2]], axis=0)
    return query_grads, key_grads, value_grads
```

```python
import functools
import math

import jax
import jax.numpy as jnp
from jax import lax
from jax.experimental import pallas as pl
from jax.experimental.pallas import tpu as pltpu
from jax.sharding import PartitionSpec as P

HEADS = 8
DIM = 128
ROWS = 128
CHUNK = 256
WIDE = 512
NEG = -1e30
MESH = pl.DeviceIdType.MESH
SCALE = 1.0 / math.sqrt(DIM)
LOG2E = 1.4426950408889634
NT = (((1,), (1,)), ((), ()))
NN = (((1,), (0,)), ((), ()))


def mm(a, b, dims=NN):
    return lax.dot_general(a, b, dims, preferred_element_type=jnp.float32)


def offsets_of(chips):
    out = [0]
    for d in range(1, chips // 2):
        out += [d, -d]
    return out + [chips // 2]


def kernel(
    chips,
    sections,
    order_ref,
    q_ref,
    g_ref,
    k_ref,
    v_ref,
    ek_ref,
    ev_ref,
    ka_ref,
    va_ref,
    dq_ref,
    dk_ref,
    dv_ref,
    qb,
    gb,
    kb,
    vb,
    kt,
    eb,
    db,
    mst,
    lst,
    dsum,
    fst,
    st_out,
    st_in,
    pbuf,
    sbuf,
    acc,
    dqt,
    dq_in,
    rs_out,
    rs_in,
    acc_own,
    acc_in,
    load_sem,
    kv_sem,
    xs,
    xr,
    ags,
    agr,
    sts,
    stv,
    dqs,
    dqr,
    rss,
    rsr,
    cs,
    cr,
    acc_sem,
):
    offsets = offsets_of(chips)
    split = [(0, 3), (3, 5), (5, 8)] if chips == 8 else [(0, 3), (3, 4)]
    sec = lax.axis_index("section")
    cx = lax.axis_index("ctx")
    chip = cx // 2
    core = lax.rem(cx, 2)
    prev = lax.rem(sec + sections - 1, sections)
    nxt = lax.rem(sec + 1, sections)
    partner = (sec, chip * 2 + 1 - core)

    def peer(section, offset):
        return (section, lax.rem(chip + offset + chips, chips) * 2 + core)

    barrier = pltpu.get_barrier_semaphore()
    for off in offsets[1:]:
        pl.semaphore_signal(barrier, inc=1, device_id=peer(sec, off), device_id_type=MESH)
    pl.semaphore_signal(barrier, inc=1, device_id=partner, device_id_type=MESH)
    for off in offsets:
        pl.semaphore_signal(barrier, inc=1, device_id=peer(nxt, off), device_id_type=MESH)
        pl.semaphore_signal(barrier, inc=1, device_id=peer(prev, off), device_id_type=MESH)

    def local(src, dst, sem):
        return pltpu.make_async_copy(src, dst, sem)

    def remote(src, dst, s, r, dev):
        return pltpu.make_async_remote_copy(
            src_ref=src, dst_ref=dst, send_sem=s, recv_sem=r, device_id=dev, device_id_type=MESH
        )

    own_kv = [
        local(k_ref.at[0], kb.at[0, pl.ds(0, ROWS)], kv_sem.at[0]),
        local(v_ref.at[0], vb.at[0, pl.ds(0, ROWS)], kv_sem.at[1]),
    ]
    loads = []
    for t in range(2):
        for i, (src, dst) in enumerate(((q_ref, qb), (g_ref, gb))):
            for h in range(HEADS):
                loads.append(
                    local(
                        src.at[t, 0, :, pl.ds(h * DIM, DIM)],
                        dst.at[t, core, h],
                        load_sem.at[t, i, h],
                    )
                )
    acc_loads = [
        local(ka_ref.at[0], acc_in.at[0, 0], acc_sem.at[0]),
        local(va_ref.at[0], acc_in.at[0, 1], acc_sem.at[1]),
    ]
    for cp in own_kv + loads + acc_loads:
        cp.start()

    pl.semaphore_wait(barrier, (chips - 1) + 1 + 2 * chips)

    gather = [[], []]
    for p in range(1, chips):
        dev = peer(sec, offsets[p])
        rows = pl.ds(p * ROWS, ROWS)
        gather[0].append(remote(k_ref.at[0], kb.at[0, rows], ags.at[0, p, 0], agr.at[0, p, 0], dev))
        gather[0].append(remote(v_ref.at[0], vb.at[0, rows], ags.at[0, p, 1], agr.at[0, p, 1], dev))
    for cp in gather[0]:
        cp.start()

    swaps = [[], []]
    for t in range(2):
        for i, (src, dst) in enumerate(((q_ref, qb), (g_ref, gb))):
            for h in range(HEADS):
                swaps[t].append(
                    remote(
                        src.at[t, 0, :, pl.ds(h * DIM, DIM)],
                        dst.at[t, core, h],
                        xs.at[t, i, h],
                        xr.at[t, i, h],
                        partner,
                    )
                )
    for cp in swaps[0]:
        cp.start()

    def next_gather(k_src, v_src):
        out = []
        for p in range(chips):
            dev = peer(prev, offsets[p])
            rows = pl.ds(p * ROWS, ROWS)
            out.append(remote(k_src, kb.at[1, rows], ags.at[1, p, 0], agr.at[1, p, 0], dev))
            out.append(remote(v_src, vb.at[1, rows], ags.at[1, p, 1], agr.at[1, p, 1], dev))
        return out

    @pl.when(sec > 0)
    def _():
        for cp in next_gather(k_ref.at[0], v_ref.at[0]):
            cp.start()

    @pl.when(sec == 0)
    def _():
        for cp in next_gather(ek_ref, ev_ref):
            cp.start()

    gather[1] = next_gather(k_ref.at[0], v_ref.at[0])
    for cp in swaps[1]:
        cp.start()
    for cp in own_kv + loads + acc_loads:
        cp.wait()

    c_exp = SCALE * LOG2E
    diff = lax.broadcasted_iota(jnp.int32, (ROWS, CHUNK), 0) - lax.rem(
        lax.broadcasted_iota(jnp.int32, (ROWS, CHUNK), 1), ROWS
    )
    total = 2 * HEADS * ROWS

    def key_group(p):
        return order_ref[lax.rem(chip - offsets[p] + chips, chips) * 2 + core]

    def first_pass(t, a, b):
        keys = kb[t, pl.ds(a * ROWS, (b - a) * ROWS), :]
        values = vb[t, pl.ds(a * ROWS, (b - a) * ROWS), :]

        @pl.loop(0, total // CHUNK)
        def _(j):
            half = j // (HEADS // 2)
            pair = pl.ds(lax.rem(j, HEADS // 2) * 2, 2)
            qs = qb[t, half, pair].reshape(CHUNK, DIM)
            gs = gb[t, half, pair].reshape(CHUNK, DIM)
            lanes = pl.ds(pl.multiple_of(j * CHUNK, CHUNK), CHUNK)
            s_all = mm(keys, qs, NT)
            d_all = mm(values, gs, NT)
            query_group = order_ref[chip * 2 + half]
            for p in range(a, b):
                part = slice((p - a) * ROWS, (p - a + 1) * ROWS)
                limit = (query_group - key_group(p)) * ROWS
                s = jnp.where(diff <= limit, s_all[part], NEG)
                m = jnp.max(s, axis=0, keepdims=True)
                e = jnp.exp2((s - m) * c_exp)
                d = d_all[part]
                eb[pl.ds(p * ROWS, ROWS), lanes] = e
                db[pl.ds(p * ROWS, ROWS), lanes] = d
                mst[pl.ds(p, 1), lanes] = m
                lst[pl.ds(p, 1), lanes] = jnp.sum(e, axis=0, keepdims=True)
                dsum[pl.ds(p, 1), lanes] = jnp.sum(e * d, axis=0, keepdims=True)

    def stats(t):
        m_b = mst[...]
        m_own = jnp.max(m_b, axis=0, keepdims=True)
        w = jnp.exp2((m_b - m_own) * c_exp)
        l_own = jnp.sum(lst[...] * w, axis=0, keepdims=True)
        d_own = jnp.sum(dsum[...] * w, axis=0, keepdims=True)
        row = lax.broadcasted_iota(jnp.int32, (8, total), 0)
        st_out[t] = jnp.where(row == 0, m_own, jnp.where(row == 1, l_own, d_own))
        cp = remote(st_out.at[t], st_in.at[t], sts.at[t], stv.at[t], partner)
        cp.start()
        cp.wait()
        m_far = st_in[t, 0:1, :]
        m = jnp.maximum(m_own, m_far)
        w_own = jnp.exp2((m_own - m) * c_exp)
        w_far = jnp.exp2((m_far - m) * c_exp)
        inv = 1.0 / (l_own * w_own + st_in[t, 1:2, :] * w_far)
        delta = (d_own * w_own + st_in[t, 2:3, :] * w_far) * inv
        fst[0] = jnp.exp2((m_b - m) * c_exp) * inv
        fst[1] = jnp.broadcast_to(delta, (chips, total))

    def second_pass(t, a, b, first):
        m_rows = (b - a) * ROWS
        acc[...] = jnp.zeros_like(acc)

        @pl.loop(0, total // WIDE)
        def _(j):
            lanes = pl.ds(pl.multiple_of(j * WIDE, WIDE), WIDE)
            half = j // (HEADS // 4)
            group = pl.ds(lax.rem(j, HEADS // 4) * 4, 4)
            delta = fst[1, 0:1, lanes]
            for p in range(a, b):
                prob = eb[pl.ds(p * ROWS, ROWS), lanes] * fst[0, p : p + 1, lanes]
                ds = prob * (db[pl.ds(p * ROWS, ROWS), lanes] - delta)
                pbuf[pl.ds((p - a) * ROWS, ROWS), :] = prob.astype(jnp.bfloat16)
                sbuf[pl.ds((p - a) * ROWS, ROWS), :] = ds.astype(jnp.bfloat16)
            pr = pbuf[pl.ds(0, m_rows), :]
            sg = sbuf[pl.ds(0, m_rows), :]
            acc[0, pl.ds(0, m_rows), :] += mm(sg, qb[t, half, group].reshape(WIDE, DIM))
            acc[1, pl.ds(0, m_rows), :] += mm(pr, gb[t, half, group].reshape(WIDE, DIM))
            part = mm(kt[:, pl.ds(a * ROWS, m_rows)], sg)
            if first:
                dqt[:, lanes] = part
            else:
                dqt[:, lanes] += part

    def send_terms(t, a, b):
        out = []
        for p in range(a, b):
            rows = pl.ds((p - a) * ROWS, ROWS)
            if p == 0:
                acc_own[t, 0] = acc[0, rows, :] * SCALE
                acc_own[t, 1] = acc[1, rows, :]
            else:
                rs_out[t, p, 0] = (acc[0, rows, :] * SCALE).astype(jnp.bfloat16)
                rs_out[t, p, 1] = acc[1, rows, :].astype(jnp.bfloat16)
                cp = remote(
                    rs_out.at[t, p], rs_in.at[t, p], rss.at[t, p], rsr.at[t, p], peer(sec, -offsets[p])
                )
                cp.start()
                out.append(cp)
        return out

    def finish_queries(t, cp):
        cp.wait()
        for h in range(HEADS):
            own = pl.ds(pl.multiple_of(core * HEADS * ROWS + h * ROWS, ROWS), ROWS)
            full = (dqt[:, own] + dq_in[t, :, pl.ds(h * ROWS, ROWS)]) * SCALE
            dq_ref[t, 0, :, pl.ds(h * DIM, DIM)] = full.T.astype(jnp.bfloat16)

    def finish_terms(t, copies):
        for cp in copies:
            cp.wait()
        for i, ref in enumerate((dk_ref, dv_ref)):
            s = acc_own[t, i]
            for p in range(1, chips):
                s = s + rs_in[t, p, i].astype(jnp.float32)
            acc_own[t, i] = s

    carry = remote(acc_own.at[0], acc_in.at[1], cs.at[0], cr.at[0], (prev, cx))
    sends = [[], []]
    for t in range(2):
        for cp in swaps[t]:
            cp.wait_recv()
        for a, b in split:
            for p in range(a, b):
                if t == 1 or p > 0:
                    for i in range(2):
                        gather[t][2 * (p - 1 + t) + i].wait_recv()
            for p in range(a, b):
                kt[:, pl.ds(p * ROWS, ROWS)] = kb[t, pl.ds(p * ROWS, ROWS), :].astype(jnp.float32).T.astype(
                    jnp.bfloat16
                )
            first_pass(t, a, b)
        stats(t)
        for n, (a, b) in enumerate(reversed(split)):
            second_pass(t, a, b, n == 0)
            sends[t] += send_terms(t, a, b)
        far = pl.ds(pl.multiple_of((1 - core) * HEADS * ROWS, HEADS * ROWS), HEADS * ROWS)
        dq_copy = remote(dqt.at[:, far], dq_in.at[t], dqs.at[t], dqr.at[t], partner)
        dq_copy.start()
        finish_queries(t, dq_copy)
        if t == 0:
            finish_terms(0, sends[0])
            acc_own[0] = acc_own[0] + acc_in[0]
            dk_ref[0, 0] = acc_own[0, 0]
            dv_ref[0, 0] = acc_own[0, 1]

            @pl.when(sec > 0)
            def _():
                carry.start()

    finish_terms(1, sends[1])

    @pl.when(sec < sections - 1)
    def _():
        carry.wait_recv()
        acc_own[1] = acc_own[1] + acc_in[1]

    dk_ref[1, 0] = acc_own[1, 0]
    dv_ref[1, 0] = acc_own[1, 1]

    @pl.when(sec > 0)
    def _():
        carry.wait_send()

    for t in range(2):
        for cp in gather[t] + swaps[t]:
            cp.wait_send()


def body(queries, out_grad, keys, values, entering_keys, entering_values, key_grads_in, value_grads_in, group_order, *, chips, sections):
    any_spec = pl.BlockSpec(memory_space=pl.ANY)
    vmem = pl.BlockSpec(memory_space=pltpu.VMEM)
    total = 2 * HEADS * ROWS
    bf16, f32 = jnp.bfloat16, jnp.float32
    dma = pltpu.SemaphoreType.DMA
    return pl.pallas_call(
        functools.partial(kernel, chips, sections),
        out_shape=(
            jax.ShapeDtypeStruct((2, 1, ROWS, HEADS * DIM), bf16),
            jax.ShapeDtypeStruct((2, 1, ROWS, DIM), f32),
            jax.ShapeDtypeStruct((2, 1, ROWS, DIM), f32),
        ),
        in_specs=[pl.BlockSpec(memory_space=pltpu.SMEM)] + [any_spec] * 8,
        out_specs=(vmem, vmem, vmem),
        scratch_shapes=[
            pltpu.VMEM((2, 2, HEADS, ROWS, DIM), bf16),
            pltpu.VMEM((2, 2, HEADS, ROWS, DIM), bf16),
            pltpu.VMEM((2, chips * ROWS, DIM), bf16),
            pltpu.VMEM((2, chips * ROWS, DIM), bf16),
            pltpu.VMEM((DIM, chips * ROWS), bf16),
            pltpu.VMEM((chips * ROWS, total), f32),
            pltpu.VMEM((chips * ROWS, total), f32),
            pltpu.VMEM((chips, total), f32),
            pltpu.VMEM((chips, total), f32),
            pltpu.VMEM((chips, total), f32),
            pltpu.VMEM((2, chips, total), f32),
            pltpu.VMEM((2, 8, total), f32),
            pltpu.VMEM((2, 8, total), f32),
            pltpu.VMEM((3 * ROWS, WIDE), bf16),
            pltpu.VMEM((3 * ROWS, WIDE), bf16),
            pltpu.VMEM((2, 3 * ROWS, DIM), f32),
            pltpu.VMEM((DIM, total), f32),
            pltpu.VMEM((2, DIM, total // 2), f32),
            pltpu.VMEM((2, chips, 2, ROWS, DIM), bf16),
            pltpu.VMEM((2, chips, 2, ROWS, DIM), bf16),
            pltpu.VMEM((2, 2, ROWS, DIM), f32),
            pltpu.VMEM((2, 2, ROWS, DIM), f32),
            dma((2, 2, HEADS)),
            dma((2,)),
            dma((2, 2, HEADS)),
            dma((2, 2, HEADS)),
            dma((2, chips, 2)),
            dma((2, chips, 2)),
            dma((2,)),
            dma((2,)),
            dma((2,)),
            dma((2,)),
            dma((2, chips)),
            dma((2, chips)),
            dma((1,)),
            dma((1,)),
            dma((2,)),
        ],
        compiler_params=pltpu.CompilerParams(
            collective_id=0, has_side_effects=True, vmem_limit_bytes=60 << 20
        ),
    )(group_order, queries, out_grad, keys, values, entering_keys, entering_values, key_grads_in, value_grads_in)


def solution(mesh):
    sections = mesh.shape["section"]
    chips = mesh.shape["ctx"] // 2
    return jax.shard_map(
        functools.partial(body, chips=chips, sections=sections),
        mesh=mesh,
        in_specs=(
            P(None, "section", "ctx", None),
            P(None, "section", "ctx", None),
            P("section", "ctx", None),
            P("section", "ctx", None),
            P("ctx", None),
            P("ctx", None),
            P("section", "ctx", None),
            P("section", "ctx", None),
            P(),
        ),
        out_specs=(
            P(None, "section", "ctx", None),
            P(None, "section", "ctx", None),
            P(None, "section", "ctx", None),
        ),
        check_vma=False,
    )
```

```python
import functools
import math

import jax
import jax.numpy as jnp
from jax import lax
from jax.experimental import pallas as pl
from jax.experimental.pallas import tpu as pltpu
from jax.sharding import PartitionSpec as P

HEADS = 8
DIM = 128
ROWS = 128
CHUNK = 256
WIDE = 512
NEG = -1e30
MESH = pl.DeviceIdType.MESH
SCALE = 1.0 / math.sqrt(DIM)
LOG2E = 1.4426950408889634
NT = (((1,), (1,)), ((), ()))
NN = (((1,), (0,)), ((), ()))


def mm(a, b, dims=NN):
    return lax.dot_general(a, b, dims, preferred_element_type=jnp.float32)


OFFSETS = (0, 1, -1, 2, -2, 3, -3, 4)
CHIPS = len(OFFSETS)
NEAR = (3, 4, 1, 2)


def kernel(
    sections,
    order_ref,
    q_ref,
    g_ref,
    k_ref,
    v_ref,
    ek_ref,
    ev_ref,
    ka_ref,
    va_ref,
    dq_ref,
    dk_ref,
    dv_ref,
    qb,
    gb,
    kb,
    vb,
    kt,
    eb,
    db,
    mst,
    lst,
    dsum,
    fst,
    st_out,
    st_in,
    pbuf,
    sbuf,
    acc,
    dqt,
    dq_in,
    rs_out,
    rs_in,
    rs_mid,
    rs_far,
    mid_own,
    acc_own,
    acc_in,
    load_sem,
    kv_sem,
    xs,
    xr,
    ags,
    agr,
    sts,
    stv,
    dqs,
    dqr,
    rss,
    rsr,
    cs,
    cr,
    acc_sem,
):
    sec = lax.axis_index("section")
    cx = lax.axis_index("ctx")
    chip = cx // 2
    core = lax.rem(cx, 2)
    prev = lax.rem(sec + sections - 1, sections)
    nxt = lax.rem(sec + 1, sections)
    partner = (sec, chip * 2 + 1 - core)

    def peer(section, offset):
        return (section, lax.rem(chip + offset + CHIPS, CHIPS) * 2 + core)

    barrier = pltpu.get_barrier_semaphore()
    for p in range(1, 5):
        pl.semaphore_signal(barrier, inc=1, device_id=peer(sec, OFFSETS[p]), device_id_type=MESH)
    pl.semaphore_signal(barrier, inc=1, device_id=partner, device_id_type=MESH)
    for p in range(5):
        pl.semaphore_signal(barrier, inc=1, device_id=peer(nxt, OFFSETS[p]), device_id_type=MESH)
        pl.semaphore_signal(barrier, inc=1, device_id=peer(prev, OFFSETS[p]), device_id_type=MESH)

    def local(src, dst, sem):
        return pltpu.make_async_copy(src, dst, sem)

    def remote(src, dst, s, r, dev):
        return pltpu.make_async_remote_copy(
            src_ref=src, dst_ref=dst, send_sem=s, recv_sem=r, device_id=dev, device_id_type=MESH
        )

    own_kv = [
        local(k_ref.at[0], kb.at[0, pl.ds(0, ROWS)], kv_sem.at[0]),
        local(v_ref.at[0], vb.at[0, pl.ds(0, ROWS)], kv_sem.at[1]),
    ]
    loads = []
    for t in range(2):
        for i, (src, dst) in enumerate(((q_ref, qb), (g_ref, gb))):
            for h in range(HEADS):
                loads.append(
                    local(
                        src.at[t, 0, :, pl.ds(h * DIM, DIM)],
                        dst.at[t, core, h],
                        load_sem.at[t, i, h],
                    )
                )
    acc_loads = [
        local(ka_ref.at[0], acc_in.at[0, 0], acc_sem.at[0]),
        local(va_ref.at[0], acc_in.at[0, 1], acc_sem.at[1]),
    ]
    for cp in own_kv + loads + acc_loads:
        cp.start()

    pl.semaphore_wait(barrier, 15)

    def kv_copies(t, p, dev, k_src, v_src):
        rows = pl.ds(p * ROWS, ROWS)
        return [
            remote(k_src, kb.at[t, rows], ags.at[t, p, 0], agr.at[t, p, 0], dev),
            remote(v_src, vb.at[t, rows], ags.at[t, p, 1], agr.at[t, p, 1], dev),
        ]

    gather = [{}, {}]
    for p in NEAR:
        gather[0][p] = kv_copies(0, p, peer(sec, OFFSETS[p]), k_ref.at[0], v_ref.at[0])
        for cp in gather[0][p]:
            cp.start()

    swaps = [[], []]
    for t in range(2):
        for i, (src, dst) in enumerate(((q_ref, qb), (g_ref, gb))):
            for h in range(HEADS):
                swaps[t].append(
                    remote(
                        src.at[t, 0, :, pl.ds(h * DIM, DIM)],
                        dst.at[t, core, h],
                        xs.at[t, i, h],
                        xr.at[t, i, h],
                        partner,
                    )
                )
    for cp in swaps[0]:
        cp.start()

    def next_gather(k_src, v_src):
        return {p: kv_copies(1, p, peer(prev, OFFSETS[p]), k_src, v_src) for p in NEAR + (0,)}

    def start_next_gather():
        @pl.when(sec > 0)
        def _():
            for cps in next_gather(k_ref.at[0], v_ref.at[0]).values():
                for cp in cps:
                    cp.start()

        @pl.when(sec == 0)
        def _():
            for cps in next_gather(ek_ref, ev_ref).values():
                for cp in cps:
                    cp.start()

        gather[1].update(next_gather(k_ref.at[0], v_ref.at[0]))

    def relay_gather(t):
        for p, near, far in ((3, 1, 5), (4, 2, 6)):
            for cp in gather[t][p]:
                cp.wait_recv()
            rows = pl.ds(p * ROWS, ROWS)
            k_src, v_src = kb.at[t, rows], vb.at[t, rows]
            gather[t][far] = kv_copies(t, far, peer(sec, OFFSETS[near]), k_src, v_src)
            for cp in gather[t][far]:
                cp.start()
            half = p - 3
            cp = kv_copies(t, 7, peer(sec, OFFSETS[p]), k_src, v_src)[half]
            cp.start()
            gather[t].setdefault(7, []).append(cp)

    def wait_keys(t, ps):
        for p in ps:
            for cp in gather[t].get(p, []):
                cp.wait_recv()

    for cp in swaps[1]:
        cp.start()
    for cp in own_kv + loads + acc_loads:
        cp.wait()

    c_exp = SCALE * LOG2E
    diff = lax.broadcasted_iota(jnp.int32, (ROWS, CHUNK), 0) - lax.rem(
        lax.broadcasted_iota(jnp.int32, (ROWS, CHUNK), 1), ROWS
    )
    total = 2 * HEADS * ROWS

    def key_group(p):
        return order_ref[lax.rem(chip - OFFSETS[p] + CHIPS, CHIPS) * 2 + core]

    def first_pass(t, a, b):
        keys = kb[t, pl.ds(a * ROWS, (b - a) * ROWS), :]
        values = vb[t, pl.ds(a * ROWS, (b - a) * ROWS), :]

        @pl.loop(0, total // CHUNK)
        def _(j):
            half = j // (HEADS // 2)
            pair = pl.ds(lax.rem(j, HEADS // 2) * 2, 2)
            qs = qb[t, half, pair].reshape(CHUNK, DIM)
            gs = gb[t, half, pair].reshape(CHUNK, DIM)
            lanes = pl.ds(pl.multiple_of(j * CHUNK, CHUNK), CHUNK)
            s_all = mm(keys, qs, NT)
            d_all = mm(values, gs, NT)
            query_group = order_ref[chip * 2 + half]
            for p in range(a, b):
                part = slice((p - a) * ROWS, (p - a + 1) * ROWS)
                limit = (query_group - key_group(p)) * ROWS
                s = jnp.where(diff <= limit, s_all[part], NEG)
                m = jnp.max(s, axis=0, keepdims=True)
                e = jnp.exp2((s - m) * c_exp)
                d = d_all[part]
                eb[pl.ds(p * ROWS, ROWS), lanes] = e
                db[pl.ds(p * ROWS, ROWS), lanes] = d
                mst[pl.ds(p, 1), lanes] = m
                lst[pl.ds(p, 1), lanes] = jnp.sum(e, axis=0, keepdims=True)
                dsum[pl.ds(p, 1), lanes] = jnp.sum(e * d, axis=0, keepdims=True)

    def stats(t):
        m_b = mst[...]
        m_own = jnp.max(m_b, axis=0, keepdims=True)
        w = jnp.exp2((m_b - m_own) * c_exp)
        l_own = jnp.sum(lst[...] * w, axis=0, keepdims=True)
        d_own = jnp.sum(dsum[...] * w, axis=0, keepdims=True)
        row = lax.broadcasted_iota(jnp.int32, (8, total), 0)
        st_out[t] = jnp.where(row == 0, m_own, jnp.where(row == 1, l_own, d_own))
        cp = remote(st_out.at[t], st_in.at[t], sts.at[t], stv.at[t], partner)
        cp.start()
        cp.wait()
        m_far = st_in[t, 0:1, :]
        m = jnp.maximum(m_own, m_far)
        w_own = jnp.exp2((m_own - m) * c_exp)
        w_far = jnp.exp2((m_far - m) * c_exp)
        inv = 1.0 / (l_own * w_own + st_in[t, 1:2, :] * w_far)
        delta = (d_own * w_own + st_in[t, 2:3, :] * w_far) * inv
        fst[0] = jnp.exp2((m_b - m) * c_exp) * inv
        fst[1] = jnp.broadcast_to(delta, (CHIPS, total))

    def second_pass(t, a, b, first):
        m_rows = (b - a) * ROWS
        acc[...] = jnp.zeros_like(acc)

        @pl.loop(0, total // WIDE)
        def _(j):
            lanes = pl.ds(pl.multiple_of(j * WIDE, WIDE), WIDE)
            half = j // (HEADS // 4)
            group = pl.ds(lax.rem(j, HEADS // 4) * 4, 4)
            delta = fst[1, 0:1, lanes]
            for p in range(a, b):
                prob = eb[pl.ds(p * ROWS, ROWS), lanes] * fst[0, p : p + 1, lanes]
                ds = prob * (db[pl.ds(p * ROWS, ROWS), lanes] - delta)
                pbuf[pl.ds((p - a) * ROWS, ROWS), :] = prob.astype(jnp.bfloat16)
                sbuf[pl.ds((p - a) * ROWS, ROWS), :] = ds.astype(jnp.bfloat16)
            pr = pbuf[pl.ds(0, m_rows), :]
            sg = sbuf[pl.ds(0, m_rows), :]
            acc[0, pl.ds(0, m_rows), :] += mm(sg, qb[t, half, group].reshape(WIDE, DIM))
            acc[1, pl.ds(0, m_rows), :] += mm(pr, gb[t, half, group].reshape(WIDE, DIM))
            part = mm(kt[:, pl.ds(a * ROWS, m_rows)], sg)
            if first:
                dqt[t, :, lanes] = part
            else:
                dqt[t, :, lanes] += part

    sends = [[], []]
    middle = [[], []]

    def push(t, src, buf, slot, sem_slot, dev, keep):
        cp = remote(src, buf.at[slot], rss.at[t, sem_slot], rsr.at[t, sem_slot], dev)
        cp.start()
        keep.append(cp)

    def send_terms(t, a, b):
        for p in range(a, b):
            rows = pl.ds((p - a) * ROWS, ROWS)
            dk = acc[0, rows, :] * SCALE
            dv = acc[1, rows, :]
            if p == 0:
                acc_own[t, 0] = dk
                acc_own[t, 1] = dv
            elif p in (3, 4):
                mid_own[p - 3, 0] = dk
                mid_own[p - 3, 1] = dv
            else:
                rs_out[t, p, 0] = dk.astype(jnp.bfloat16)
                rs_out[t, p, 1] = dv.astype(jnp.bfloat16)
                if p < 3:
                    push(t, rs_out.at[t, p], rs_in, (t, p), p, peer(sec, -OFFSETS[p]), sends[t])
                elif p < 7:
                    near = p - 4
                    push(t, rs_out.at[t, p], rs_mid, (t, p - 5), p, peer(sec, -OFFSETS[near]), middle[t])
                else:
                    push(t, rs_out.at[t, p, 0], rs_far, (t, 0), 7, peer(sec, -2), middle[t])
                    push(t, rs_out.at[t, p, 1], rs_far, (t, 1), 0, peer(sec, 2), middle[t])

    def relay_terms(t):
        for cp in middle[t]:
            cp.wait_recv()
        for p in (3, 4):
            n = p - 3
            dk = mid_own[n, 0] + rs_mid[t, n, 0].astype(jnp.float32)
            dv = mid_own[n, 1] + rs_mid[t, n, 1].astype(jnp.float32)
            far = rs_far[t, n].astype(jnp.float32)
            if n == 0:
                dk = dk + far
            else:
                dv = dv + far
            rs_out[t, p, 0] = dk.astype(jnp.bfloat16)
            rs_out[t, p, 1] = dv.astype(jnp.bfloat16)
            push(t, rs_out.at[t, p], rs_in, (t, p), p, peer(sec, -OFFSETS[p]), sends[t])

    far_rows = pl.ds(pl.multiple_of((1 - core) * HEADS * ROWS, HEADS * ROWS), HEADS * ROWS)
    dq_copies = [
        remote(dqt.at[t, :, far_rows], dq_in.at[t], dqs.at[t], dqr.at[t], partner) for t in range(2)
    ]

    def finish_queries(t):
        dq_copies[t].wait()
        for h in range(HEADS):
            own = pl.ds(pl.multiple_of(core * HEADS * ROWS + h * ROWS, ROWS), ROWS)
            full = (dqt[t, :, own] + dq_in[t, :, pl.ds(h * ROWS, ROWS)]) * SCALE
            dq_ref[t, 0, :, pl.ds(h * DIM, DIM)] = full.T.astype(jnp.bfloat16)

    def finish_terms(t):
        for cp in sends[t]:
            cp.wait_recv()
        for i in range(2):
            s = acc_own[t, i]
            for p in range(1, 5):
                s = s + rs_in[t, p, i].astype(jnp.float32)
            if t == 0:
                s = s + acc_in[0, i]
            acc_own[t, i] = s

    carry = remote(acc_own.at[0], acc_in.at[1], cs.at[0], cr.at[0], (prev, cx))
    def make_transposed(t):
        for p in range(CHIPS):
            rows = pl.ds(p * ROWS, ROWS)
            kt[:, rows] = kb[t, rows, :].astype(jnp.float32).T.astype(jnp.bfloat16)

    def swap_wait(t):
        for cp in swaps[t]:
            cp.wait_recv()

    def all_second(t):
        for n, (a, b) in enumerate(((5, 8), (0, 3), (3, 5))):
            second_pass(t, a, b, n == 0)
            send_terms(t, a, b)
        dq_copies[t].start()

    swap_wait(0)
    first_pass(0, 0, 1)
    relay_gather(0)
    start_next_gather()
    wait_keys(0, (1, 2))
    first_pass(0, 1, 5)
    wait_keys(0, (5, 6, 7))
    first_pass(0, 5, 8)
    make_transposed(0)
    stats(0)
    all_second(0)

    relay_gather(1)
    swap_wait(1)
    wait_keys(1, (0, 1, 2))
    first_pass(1, 0, 5)
    relay_terms(0)
    wait_keys(1, (5, 6, 7))
    first_pass(1, 5, 8)
    make_transposed(1)
    finish_queries(0)
    finish_terms(0)
    dk_ref[0, 0] = acc_own[0, 0]
    dv_ref[0, 0] = acc_own[0, 1]

    @pl.when(sec > 0)
    def _():
        carry.start()

    stats(1)
    all_second(1)
    relay_terms(1)
    finish_queries(1)
    finish_terms(1)

    @pl.when(sec < sections - 1)
    def _():
        carry.wait_recv()
        acc_own[1] = acc_own[1] + acc_in[1]

    dk_ref[1, 0] = acc_own[1, 0]
    dv_ref[1, 0] = acc_own[1, 1]

    @pl.when(sec > 0)
    def _():
        carry.wait_send()

    for t in range(2):
        for cps in gather[t].values():
            for cp in cps:
                cp.wait_send()
        for cp in swaps[t] + middle[t] + sends[t]:
            cp.wait_send()


def body(queries, out_grad, keys, values, entering_keys, entering_values, key_grads_in, value_grads_in, group_order, *, sections):
    any_spec = pl.BlockSpec(memory_space=pl.ANY)
    vmem = pl.BlockSpec(memory_space=pltpu.VMEM)
    total = 2 * HEADS * ROWS
    bf16, f32 = jnp.bfloat16, jnp.float32
    dma = pltpu.SemaphoreType.DMA
    return pl.pallas_call(
        functools.partial(kernel, sections),
        out_shape=(
            jax.ShapeDtypeStruct((2, 1, ROWS, HEADS * DIM), bf16),
            jax.ShapeDtypeStruct((2, 1, ROWS, DIM), f32),
            jax.ShapeDtypeStruct((2, 1, ROWS, DIM), f32),
        ),
        in_specs=[pl.BlockSpec(memory_space=pltpu.SMEM)] + [any_spec] * 8,
        out_specs=(vmem, vmem, vmem),
        scratch_shapes=[
            pltpu.VMEM((2, 2, HEADS, ROWS, DIM), bf16),
            pltpu.VMEM((2, 2, HEADS, ROWS, DIM), bf16),
            pltpu.VMEM((2, CHIPS * ROWS, DIM), bf16),
            pltpu.VMEM((2, CHIPS * ROWS, DIM), bf16),
            pltpu.VMEM((DIM, CHIPS * ROWS), bf16),
            pltpu.VMEM((CHIPS * ROWS, total), f32),
            pltpu.VMEM((CHIPS * ROWS, total), f32),
            pltpu.VMEM((CHIPS, total), f32),
            pltpu.VMEM((CHIPS, total), f32),
            pltpu.VMEM((CHIPS, total), f32),
            pltpu.VMEM((2, CHIPS, total), f32),
            pltpu.VMEM((2, 8, total), f32),
            pltpu.VMEM((2, 8, total), f32),
            pltpu.VMEM((3 * ROWS, WIDE), bf16),
            pltpu.VMEM((3 * ROWS, WIDE), bf16),
            pltpu.VMEM((2, 3 * ROWS, DIM), f32),
            pltpu.VMEM((2, DIM, total), f32),
            pltpu.VMEM((2, DIM, total // 2), f32),
            pltpu.VMEM((2, CHIPS, 2, ROWS, DIM), bf16),
            pltpu.VMEM((2, 5, 2, ROWS, DIM), bf16),
            pltpu.VMEM((2, 2, 2, ROWS, DIM), bf16),
            pltpu.VMEM((2, 2, ROWS, DIM), bf16),
            pltpu.VMEM((2, 2, ROWS, DIM), f32),
            pltpu.VMEM((2, 2, ROWS, DIM), f32),
            pltpu.VMEM((2, 2, ROWS, DIM), f32),
            dma((2, 2, HEADS)),
            dma((2,)),
            dma((2, 2, HEADS)),
            dma((2, 2, HEADS)),
            dma((2, CHIPS, 2)),
            dma((2, CHIPS, 2)),
            dma((2,)),
            dma((2,)),
            dma((2,)),
            dma((2,)),
            dma((2, CHIPS)),
            dma((2, CHIPS)),
            dma((1,)),
            dma((1,)),
            dma((2,)),
        ],
        compiler_params=pltpu.CompilerParams(
            collective_id=0, has_side_effects=True, vmem_limit_bytes=60 << 20
        ),
    )(group_order, queries, out_grad, keys, values, entering_keys, entering_values, key_grads_in, value_grads_in)


def solution(mesh):
    sections = mesh.shape["section"]
    return jax.shard_map(
        functools.partial(body, sections=sections),
        mesh=mesh,
        in_specs=(
            P(None, "section", "ctx", None),
            P(None, "section", "ctx", None),
            P("section", "ctx", None),
            P("section", "ctx", None),
            P("ctx", None),
            P("ctx", None),
            P("section", "ctx", None),
            P("section", "ctx", None),
            P(),
        ),
        out_specs=(
            P(None, "section", "ctx", None),
            P(None, "section", "ctx", None),
            P(None, "section", "ctx", None),
        ),
        check_vma=False,
    )
```

```python
import functools
import math

import jax
import jax.numpy as jnp
from jax import lax
from jax.experimental import pallas as pl
from jax.experimental.pallas import tpu as pltpu
from jax.sharding import PartitionSpec as P

HEADS = 8
DIM = 128
ROWS = 128
CHUNK = 256
WIDE = 512
UNROLL = 2
UNROLL2 = 2
NEG = -1e30
MESH = pl.DeviceIdType.MESH
SCALE = 1.0 / math.sqrt(DIM)
LOG2E = 1.4426950408889634
NT = (((1,), (1,)), ((), ()))
NN = (((1,), (0,)), ((), ()))


def mm(a, b, dims=NN):
    return lax.dot_general(a, b, dims, preferred_element_type=jnp.float32)


OFFSETS = (0, 1, -1, 2, -2, 3, -3, 4)
CHIPS = len(OFFSETS)
NEAR = (3, 4, 1, 2)


def kernel(
    sections,
    order_ref,
    q_ref,
    g_ref,
    k_ref,
    v_ref,
    ek_ref,
    ev_ref,
    ka_ref,
    va_ref,
    dq_ref,
    dk_ref,
    dv_ref,
    qb,
    gb,
    kb,
    vb,
    kt,
    eb,
    db,
    mst,
    lst,
    dsum,
    fst,
    st_out,
    st_in,
    pbuf,
    sbuf,
    acc,
    dqt,
    dq_in,
    rs_out,
    rs_in,
    rs_mid,
    rs_far,
    mid_own,
    acc_own,
    acc_in,
    load_sem,
    kv_sem,
    xs,
    xr,
    ags,
    agr,
    sts,
    stv,
    dqs,
    dqr,
    rss,
    rsr,
    cs,
    cr,
    acc_sem,
):
    sec = lax.axis_index("section")
    cx = lax.axis_index("ctx")
    chip = cx // 2
    core = lax.rem(cx, 2)
    prev = lax.rem(sec + sections - 1, sections)
    nxt = lax.rem(sec + 1, sections)
    partner = (sec, chip * 2 + 1 - core)

    def peer(section, offset):
        return (section, lax.rem(chip + offset + CHIPS, CHIPS) * 2 + core)

    barrier = pltpu.get_barrier_semaphore()
    for p in range(1, 5):
        pl.semaphore_signal(barrier, inc=1, device_id=peer(sec, OFFSETS[p]), device_id_type=MESH)
    pl.semaphore_signal(barrier, inc=1, device_id=partner, device_id_type=MESH)
    pl.semaphore_signal(barrier, inc=1, device_id=(nxt, cx), device_id_type=MESH)
    pl.semaphore_signal(barrier, inc=1, device_id=(prev, cx), device_id_type=MESH)

    def local(src, dst, sem):
        return pltpu.make_async_copy(src, dst, sem)

    def remote(src, dst, s, r, dev):
        return pltpu.make_async_remote_copy(
            src_ref=src, dst_ref=dst, send_sem=s, recv_sem=r, device_id=dev, device_id_type=MESH
        )

    own_kv = [
        local(k_ref.at[0], kb.at[0, pl.ds(0, ROWS)], kv_sem.at[0]),
        local(v_ref.at[0], vb.at[0, pl.ds(0, ROWS)], kv_sem.at[1]),
    ]
    loads = []
    for t in range(2):
        for i, (src, dst) in enumerate(((q_ref, qb), (g_ref, gb))):
            for h in range(HEADS):
                loads.append(
                    local(
                        src.at[t, 0, :, pl.ds(h * DIM, DIM)],
                        dst.at[t, core, h],
                        load_sem.at[t, i, h],
                    )
                )
    acc_loads = [
        local(ka_ref.at[0], acc_in.at[0, 0], acc_sem.at[0]),
        local(va_ref.at[0], acc_in.at[0, 1], acc_sem.at[1]),
    ]
    for cp in own_kv + loads + acc_loads:
        cp.start()

    pl.semaphore_wait(barrier, 7)

    def kv_copies(t, p, dev, k_src, v_src):
        rows = pl.ds(p * ROWS, ROWS)
        return [
            remote(k_src, kb.at[t, rows], ags.at[t, p, 0], agr.at[t, p, 0], dev),
            remote(v_src, vb.at[t, rows], ags.at[t, p, 1], agr.at[t, p, 1], dev),
        ]

    gather = [{}, {}]
    for p in NEAR:
        gather[0][p] = kv_copies(0, p, peer(sec, OFFSETS[p]), k_ref.at[0], v_ref.at[0])
        for cp in gather[0][p]:
            cp.start()

    swaps = [[], []]
    for t in range(2):
        for i, (src, dst) in enumerate(((q_ref, qb), (g_ref, gb))):
            for h in range(HEADS):
                swaps[t].append(
                    remote(
                        src.at[t, 0, :, pl.ds(h * DIM, DIM)],
                        dst.at[t, core, h],
                        xs.at[t, i, h],
                        xr.at[t, i, h],
                        partner,
                    )
                )
    for cp in swaps[0]:
        cp.start()

    def shift_keys(k_src, v_src):
        return kv_copies(1, 0, (prev, cx), k_src, v_src)

    @pl.when(sec > 0)
    def _():
        for cp in shift_keys(k_ref.at[0], v_ref.at[0]):
            cp.start()

    @pl.when(sec == 0)
    def _():
        for cp in shift_keys(ek_ref, ev_ref):
            cp.start()

    gather[1][0] = shift_keys(k_ref.at[0], v_ref.at[0])

    def start_next_gather():
        for cp in gather[1][0]:
            cp.wait_recv()
        rows = pl.ds(0, ROWS)
        for p in NEAR:
            gather[1][p] = kv_copies(1, p, peer(sec, OFFSETS[p]), kb.at[1, rows], vb.at[1, rows])
            for cp in gather[1][p]:
                cp.start()

    def relay_gather(t):
        for p, near, far in ((3, 1, 5), (4, 2, 6)):
            for cp in gather[t][p]:
                cp.wait_recv()
            rows = pl.ds(p * ROWS, ROWS)
            k_src, v_src = kb.at[t, rows], vb.at[t, rows]
            gather[t][far] = kv_copies(t, far, peer(sec, OFFSETS[near]), k_src, v_src)
            for cp in gather[t][far]:
                cp.start()
            half = p - 3
            cp = kv_copies(t, 7, peer(sec, OFFSETS[p]), k_src, v_src)[half]
            cp.start()
            gather[t].setdefault(7, []).append(cp)

    def wait_keys(t, ps):
        for p in ps:
            for cp in gather[t].get(p, []):
                cp.wait_recv()

    for cp in swaps[1]:
        cp.start()
    for cp in own_kv + loads + acc_loads:
        cp.wait()

    c_exp = SCALE * LOG2E
    diff = lax.broadcasted_iota(jnp.int32, (ROWS, CHUNK), 0) - lax.rem(
        lax.broadcasted_iota(jnp.int32, (ROWS, CHUNK), 1), ROWS
    )
    total = 2 * HEADS * ROWS

    def key_group(p):
        return order_ref[lax.rem(chip - OFFSETS[p] + CHIPS, CHIPS) * 2 + core]

    def first_pass(t, a, b):
        keys = kb[t, pl.ds(a * ROWS, (b - a) * ROWS), :]
        values = vb[t, pl.ds(a * ROWS, (b - a) * ROWS), :]

        @pl.loop(0, total // CHUNK, unroll=UNROLL)
        def _(j):
            half = j // (HEADS // 2)
            pair = pl.ds(lax.rem(j, HEADS // 2) * 2, 2)
            qs = qb[t, half, pair].reshape(CHUNK, DIM)
            gs = gb[t, half, pair].reshape(CHUNK, DIM)
            lanes = pl.ds(pl.multiple_of(j * CHUNK, CHUNK), CHUNK)
            s_all = mm(keys, qs, NT)
            d_all = mm(values, gs, NT)
            query_group = order_ref[chip * 2 + half]
            for p in range(a, b):
                part = slice((p - a) * ROWS, (p - a + 1) * ROWS)
                ahead = query_group - key_group(p)
                s = s_all[part]
                if p == 0:
                    s = jnp.where(diff <= ahead * ROWS, s, NEG)
                m = jnp.max(s, axis=0, keepdims=True)
                e = jnp.exp2((s - m) * c_exp)
                d = d_all[part]
                eb[t, pl.ds(p * ROWS, ROWS), lanes] = e
                db[t, pl.ds(p * ROWS, ROWS), lanes] = d
                if p > 0:
                    m = jnp.where(ahead > 0, m, NEG)
                mst[t, pl.ds(p, 1), lanes] = m
                lst[t, pl.ds(p, 1), lanes] = jnp.sum(e, axis=0, keepdims=True)
                dsum[t, pl.ds(p, 1), lanes] = jnp.sum(e * d, axis=0, keepdims=True)

    def stats(t, meanwhile):
        m_b = mst[t]
        m_own = jnp.max(m_b, axis=0, keepdims=True)
        w = jnp.exp2((m_b - m_own) * c_exp)
        l_own = jnp.sum(lst[t] * w, axis=0, keepdims=True)
        d_own = jnp.sum(dsum[t] * w, axis=0, keepdims=True)
        row = lax.broadcasted_iota(jnp.int32, (8, total), 0)
        st_out[t] = jnp.where(row == 0, m_own, jnp.where(row == 1, l_own, d_own))
        cp = remote(st_out.at[t], st_in.at[t], sts.at[t], stv.at[t], partner)
        cp.start()
        meanwhile()
        cp.wait()
        m_far = st_in[t, 0:1, :]
        m = jnp.maximum(m_own, m_far)
        w_own = jnp.exp2((m_own - m) * c_exp)
        w_far = jnp.exp2((m_far - m) * c_exp)
        inv = 1.0 / (l_own * w_own + st_in[t, 1:2, :] * w_far)
        delta = (d_own * w_own + st_in[t, 2:3, :] * w_far) * inv
        fst[0] = jnp.exp2((m_b - m) * c_exp) * inv
        fst[1] = jnp.broadcast_to(delta, (CHIPS, total))

    def second_pass(t, a, b):
        m_rows = (b - a) * ROWS
        acc[...] = jnp.zeros_like(acc)

        @pl.loop(0, total // WIDE, unroll=UNROLL2)
        def _(j):
            lanes = pl.ds(pl.multiple_of(j * WIDE, WIDE), WIDE)
            half = j // (HEADS // 4)
            group = pl.ds(lax.rem(j, HEADS // 4) * 4, 4)
            delta = fst[1, 0:1, lanes]
            for p in range(a, b):
                prob = eb[t, pl.ds(p * ROWS, ROWS), lanes] * fst[0, p : p + 1, lanes]
                ds = prob * (db[t, pl.ds(p * ROWS, ROWS), lanes] - delta)
                pbuf[pl.ds((p - a) * ROWS, ROWS), :] = prob.astype(jnp.bfloat16)
                sbuf[pl.ds(p * ROWS, ROWS), lanes] = ds.astype(jnp.bfloat16)
            pr = pbuf[pl.ds(0, m_rows), :]
            sg = sbuf[pl.ds(a * ROWS, m_rows), lanes]
            acc[0, pl.ds(0, m_rows), :] += mm(sg, qb[t, half, group].reshape(WIDE, DIM))
            acc[1, pl.ds(0, m_rows), :] += mm(pr, gb[t, half, group].reshape(WIDE, DIM))

    def query_terms(t):
        @pl.loop(0, total // WIDE, unroll=UNROLL2)
        def _(j):
            lanes = pl.ds(pl.multiple_of(j * WIDE, WIDE), WIDE)
            dqt[t, :, lanes] = mm(kt[t], sbuf[:, lanes])

        dq_copies[t].start()

    sends = [[], []]
    middle = [[], []]

    def push(t, src, buf, slot, sem_slot, dev, keep):
        cp = remote(src, buf.at[slot], rss.at[t, sem_slot], rsr.at[t, sem_slot], dev)
        cp.start()
        keep.append(cp)

    def send_terms(t, a, b):
        for p in range(a, b):
            rows = pl.ds((p - a) * ROWS, ROWS)
            dk = acc[0, rows, :] * SCALE
            dv = acc[1, rows, :]
            if p == 0:
                acc_own[t, 0] = dk
                acc_own[t, 1] = dv
            elif p in (3, 4):
                mid_own[p - 3, 0] = dk
                mid_own[p - 3, 1] = dv
            else:
                rs_out[t, p, 0] = dk.astype(jnp.bfloat16)
                rs_out[t, p, 1] = dv.astype(jnp.bfloat16)
                if p < 3:
                    push(t, rs_out.at[t, p], rs_in, (t, p), p, peer(sec, -OFFSETS[p]), sends[t])
                elif p < 7:
                    near = p - 4
                    push(t, rs_out.at[t, p], rs_mid, (t, p - 5), p, peer(sec, -OFFSETS[near]), middle[t])
                else:
                    push(t, rs_out.at[t, p, 0], rs_far, (t, 0), 7, peer(sec, -2), middle[t])
                    push(t, rs_out.at[t, p, 1], rs_far, (t, 1), 0, peer(sec, 2), middle[t])

    def relay_terms(t):
        for cp in middle[t]:
            cp.wait_recv()
        for p in (3, 4):
            n = p - 3
            dk = mid_own[n, 0] + rs_mid[t, n, 0].astype(jnp.float32)
            dv = mid_own[n, 1] + rs_mid[t, n, 1].astype(jnp.float32)
            far = rs_far[t, n].astype(jnp.float32)
            if n == 0:
                dk = dk + far
            else:
                dv = dv + far
            rs_out[t, p, 0] = dk.astype(jnp.bfloat16)
            rs_out[t, p, 1] = dv.astype(jnp.bfloat16)
            push(t, rs_out.at[t, p], rs_in, (t, p), p, peer(sec, -OFFSETS[p]), sends[t])

    far_rows = pl.ds(pl.multiple_of((1 - core) * HEADS * ROWS, HEADS * ROWS), HEADS * ROWS)
    dq_copies = [
        remote(dqt.at[t, :, far_rows], dq_in.at[t], dqs.at[t], dqr.at[t], partner) for t in range(2)
    ]

    def finish_queries(t):
        dq_copies[t].wait()
        for h in range(HEADS):
            own = pl.ds(pl.multiple_of(core * HEADS * ROWS + h * ROWS, ROWS), ROWS)
            full = (dqt[t, :, own] + dq_in[t, :, pl.ds(h * ROWS, ROWS)]) * SCALE
            dq_ref[t, 0, :, pl.ds(h * DIM, DIM)] = full.T.astype(jnp.bfloat16)

    def finish_terms(t):
        for cp in sends[t]:
            cp.wait_recv()
        for i in range(2):
            s = acc_own[t, i]
            for p in range(1, 5):
                s = s + rs_in[t, p, i].astype(jnp.float32)
            if t == 0:
                s = s + acc_in[0, i]
            acc_own[t, i] = s

    carry = remote(acc_own.at[0], acc_in.at[1], cs.at[0], cr.at[0], (prev, cx))
    def make_transposed(t, ps):
        for p in ps:
            rows = pl.ds(p * ROWS, ROWS)
            kt[t, :, rows] = kb[t, rows, :].astype(jnp.float32).T.astype(jnp.bfloat16)

    def swap_wait(t):
        for cp in swaps[t]:
            cp.wait_recv()

    def all_second(t):
        for a, b in ((5, 8), (0, 3), (3, 5)):
            second_pass(t, a, b)
            send_terms(t, a, b)

    def ahead():
        make_transposed(0, (5, 6, 7))
        relay_gather(1)
        wait_keys(1, (1, 2))
        first_pass(1, 1, 5)

    def between():
        relay_terms(0)
        query_terms(0)
        make_transposed(1, range(1, CHIPS))

    swap_wait(0)
    first_pass(0, 0, 1)
    make_transposed(0, (0,))
    relay_gather(0)
    start_next_gather()
    swap_wait(1)
    first_pass(1, 0, 1)
    make_transposed(1, (0,))
    wait_keys(0, (1, 2))
    first_pass(0, 1, 5)
    make_transposed(0, (1, 2, 3, 4))
    wait_keys(0, (5, 6, 7))
    first_pass(0, 5, 8)
    stats(0, ahead)
    all_second(0)
    wait_keys(1, (5, 6, 7))
    first_pass(1, 5, 8)
    stats(1, between)
    all_second(1)
    finish_terms(0)
    dk_ref[0, 0] = acc_own[0, 0]
    dv_ref[0, 0] = acc_own[0, 1]

    @pl.when(sec > 0)
    def _():
        carry.start()

    query_terms(1)
    relay_terms(1)
    finish_queries(0)
    finish_queries(1)
    finish_terms(1)

    @pl.when(sec < sections - 1)
    def _():
        carry.wait_recv()
        acc_own[1] = acc_own[1] + acc_in[1]

    dk_ref[1, 0] = acc_own[1, 0]
    dv_ref[1, 0] = acc_own[1, 1]

    @pl.when(sec > 0)
    def _():
        carry.wait_send()

    for t in range(2):
        for cps in gather[t].values():
            for cp in cps:
                cp.wait_send()
        for cp in swaps[t] + middle[t] + sends[t]:
            cp.wait_send()


def body(queries, out_grad, keys, values, entering_keys, entering_values, key_grads_in, value_grads_in, group_order, *, sections):
    arrays = (queries, out_grad, keys, values, entering_keys, entering_values, key_grads_in, value_grads_in)
    any_spec = pl.BlockSpec(memory_space=pltpu.HBM)
    vmem = pl.BlockSpec(memory_space=pltpu.VMEM)
    total = 2 * HEADS * ROWS
    bf16, f32 = jnp.bfloat16, jnp.float32
    dma = pltpu.SemaphoreType.DMA
    return pl.pallas_call(
        functools.partial(kernel, sections),
        out_shape=(
            jax.ShapeDtypeStruct((2, 1, ROWS, HEADS * DIM), bf16),
            jax.ShapeDtypeStruct((2, 1, ROWS, DIM), f32),
            jax.ShapeDtypeStruct((2, 1, ROWS, DIM), f32),
        ),
        in_specs=[pl.BlockSpec(memory_space=pltpu.SMEM)] + [any_spec] * 8,
        out_specs=(vmem, vmem, vmem),
        scratch_shapes=[
            pltpu.VMEM((2, 2, HEADS, ROWS, DIM), bf16),
            pltpu.VMEM((2, 2, HEADS, ROWS, DIM), bf16),
            pltpu.VMEM((2, CHIPS * ROWS, DIM), bf16),
            pltpu.VMEM((2, CHIPS * ROWS, DIM), bf16),
            pltpu.VMEM((2, DIM, CHIPS * ROWS), bf16),
            pltpu.VMEM((2, CHIPS * ROWS, total), f32),
            pltpu.VMEM((2, CHIPS * ROWS, total), f32),
            pltpu.VMEM((2, CHIPS, total), f32),
            pltpu.VMEM((2, CHIPS, total), f32),
            pltpu.VMEM((2, CHIPS, total), f32),
            pltpu.VMEM((2, CHIPS, total), f32),
            pltpu.VMEM((2, 8, total), f32),
            pltpu.VMEM((2, 8, total), f32),
            pltpu.VMEM((3 * ROWS, WIDE), bf16),
            pltpu.VMEM((CHIPS * ROWS, total), bf16),
            pltpu.VMEM((2, 3 * ROWS, DIM), f32),
            pltpu.VMEM((2, DIM, total), f32),
            pltpu.VMEM((2, DIM, total // 2), f32),
            pltpu.VMEM((2, CHIPS, 2, ROWS, DIM), bf16),
            pltpu.VMEM((2, 5, 2, ROWS, DIM), bf16),
            pltpu.VMEM((2, 2, 2, ROWS, DIM), bf16),
            pltpu.VMEM((2, 2, ROWS, DIM), bf16),
            pltpu.VMEM((2, 2, ROWS, DIM), f32),
            pltpu.VMEM((2, 2, ROWS, DIM), f32),
            pltpu.VMEM((2, 2, ROWS, DIM), f32),
            dma((2, 2, HEADS)),
            dma((2,)),
            dma((2, 2, HEADS)),
            dma((2, 2, HEADS)),
            dma((2, CHIPS, 2)),
            dma((2, CHIPS, 2)),
            dma((2,)),
            dma((2,)),
            dma((2,)),
            dma((2,)),
            dma((2, CHIPS)),
            dma((2, CHIPS)),
            dma((1,)),
            dma((1,)),
            dma((2,)),
        ],
        compiler_params=pltpu.CompilerParams(
            collective_id=0, has_side_effects=True, vmem_limit_bytes=49 << 20
        ),
    )(group_order, *(pltpu.with_memory_space_constraint(x, pltpu.HBM) for x in arrays))


def solution(mesh):
    sections = mesh.shape["section"]
    return jax.shard_map(
        functools.partial(body, sections=sections),
        mesh=mesh,
        in_specs=(
            P(None, "section", "ctx", None),
            P(None, "section", "ctx", None),
            P("section", "ctx", None),
            P("section", "ctx", None),
            P("ctx", None),
            P("ctx", None),
            P("section", "ctx", None),
            P("section", "ctx", None),
            P(),
        ),
        out_specs=(
            P(None, "section", "ctx", None),
            P(None, "section", "ctx", None),
            P(None, "section", "ctx", None),
        ),
        check_vma=False,
    )
```

```python
import functools
import math

import jax
import jax.numpy as jnp
from jax import lax
from jax.experimental import pallas as pl
from jax.experimental.pallas import tpu as pltpu
from jax.sharding import PartitionSpec as P

HEADS = 8
DIM = 128
ROWS = 128
CHUNK = 256
WIDE = 512
UNROLL = 4
UNROLL2 = 4
NEG = -1e30
MESH = pl.DeviceIdType.MESH
SCALE = 1.0 / math.sqrt(DIM)
LOG2E = 1.4426950408889634
NT = (((1,), (1,)), ((), ()))
NN = (((1,), (0,)), ((), ()))


def mm(a, b, dims=NN):
    return lax.dot_general(a, b, dims, preferred_element_type=jnp.float32)


OFFSETS = (0, 1, -1, 2, -2, 3, -3, 4)
CHIPS = len(OFFSETS)
NEAR = (3, 4, 1, 2)
TERMS = (((5, 8), (0, 3), (3, 5)), ((7, 8), (5, 7), (0, 3), (3, 5)))


def kernel(
    sections,
    order_ref,
    q_ref,
    g_ref,
    k_ref,
    v_ref,
    ek_ref,
    ev_ref,
    ka_ref,
    va_ref,
    dq_ref,
    dk_ref,
    dv_ref,
    qb,
    gb,
    kb,
    vb,
    kt,
    eb,
    db,
    mst,
    lst,
    dsum,
    fst,
    st_out,
    st_in,
    pbuf,
    sbuf,
    acc,
    dqt,
    dq_in,
    rs_out,
    rs_in,
    rs_mid,
    rs_far,
    mid_own,
    acc_own,
    acc_in,
    load_sem,
    kv_sem,
    xs,
    xr,
    ags,
    agr,
    sts,
    stv,
    dqs,
    dqr,
    rss,
    rsr,
    cs,
    cr,
    acc_sem,
):
    sec = lax.axis_index("section")
    cx = lax.axis_index("ctx")
    chip = cx // 2
    core = lax.rem(cx, 2)
    prev = lax.rem(sec + sections - 1, sections)
    nxt = lax.rem(sec + 1, sections)
    partner = (sec, chip * 2 + 1 - core)

    def peer(section, offset):
        return (section, lax.rem(chip + offset + CHIPS, CHIPS) * 2 + core)

    barrier = pltpu.get_barrier_semaphore()
    for p in range(1, 5):
        pl.semaphore_signal(barrier, inc=1, device_id=peer(sec, OFFSETS[p]), device_id_type=MESH)
    pl.semaphore_signal(barrier, inc=1, device_id=partner, device_id_type=MESH)
    pl.semaphore_signal(barrier, inc=1, device_id=(nxt, cx), device_id_type=MESH)
    pl.semaphore_signal(barrier, inc=1, device_id=(prev, cx), device_id_type=MESH)

    def local(src, dst, sem):
        return pltpu.make_async_copy(src, dst, sem)

    def remote(src, dst, s, r, dev):
        return pltpu.make_async_remote_copy(
            src_ref=src, dst_ref=dst, send_sem=s, recv_sem=r, device_id=dev, device_id_type=MESH
        )

    own_kv = [
        local(k_ref.at[0], kb.at[0, pl.ds(0, ROWS)], kv_sem.at[0]),
        local(v_ref.at[0], vb.at[0, pl.ds(0, ROWS)], kv_sem.at[1]),
    ]
    loads = []
    for t in range(2):
        for i, (src, dst) in enumerate(((q_ref, qb), (g_ref, gb))):
            for h in range(HEADS):
                loads.append(
                    local(
                        src.at[t, 0, :, pl.ds(h * DIM, DIM)],
                        dst.at[t, core, h],
                        load_sem.at[t, i, h],
                    )
                )
    acc_loads = [
        local(ka_ref.at[0], acc_in.at[0, 0], acc_sem.at[0]),
        local(va_ref.at[0], acc_in.at[0, 1], acc_sem.at[1]),
    ]
    for cp in own_kv + loads + acc_loads:
        cp.start()

    pl.semaphore_wait(barrier, 7)

    def kv_copies(t, p, dev, k_src, v_src):
        rows = pl.ds(p * ROWS, ROWS)
        return [
            remote(k_src, kb.at[t, rows], ags.at[t, p, 0], agr.at[t, p, 0], dev),
            remote(v_src, vb.at[t, rows], ags.at[t, p, 1], agr.at[t, p, 1], dev),
        ]

    gather = [{}, {}]
    for p in NEAR:
        gather[0][p] = kv_copies(0, p, peer(sec, OFFSETS[p]), k_ref.at[0], v_ref.at[0])
        for cp in gather[0][p]:
            cp.start()

    swaps = [[], []]
    for t in range(2):
        for i, (src, dst) in enumerate(((q_ref, qb), (g_ref, gb))):
            for h in range(HEADS):
                swaps[t].append(
                    remote(
                        src.at[t, 0, :, pl.ds(h * DIM, DIM)],
                        dst.at[t, core, h],
                        xs.at[t, i, h],
                        xr.at[t, i, h],
                        partner,
                    )
                )
    for cp in swaps[0]:
        cp.start()

    def shift_keys(k_src, v_src):
        return kv_copies(1, 0, (prev, cx), k_src, v_src)

    @pl.when(sec > 0)
    def _():
        for cp in shift_keys(k_ref.at[0], v_ref.at[0]):
            cp.start()

    @pl.when(sec == 0)
    def _():
        for cp in shift_keys(ek_ref, ev_ref):
            cp.start()

    gather[1][0] = shift_keys(k_ref.at[0], v_ref.at[0])

    def start_next_gather(ps):
        rows = pl.ds(0, ROWS)
        for p in ps:
            gather[1][p] = kv_copies(1, p, peer(sec, OFFSETS[p]), kb.at[1, rows], vb.at[1, rows])
            for cp in gather[1][p]:
                cp.start()

    def relay_gather(t):
        for p, near, far in ((3, 1, 5), (4, 2, 6)):
            for cp in gather[t][p]:
                cp.wait_recv()
            rows = pl.ds(p * ROWS, ROWS)
            k_src, v_src = kb.at[t, rows], vb.at[t, rows]
            gather[t][far] = kv_copies(t, far, peer(sec, OFFSETS[near]), k_src, v_src)
            for cp in gather[t][far]:
                cp.start()
            half = p - 3
            cp = kv_copies(t, 7, peer(sec, OFFSETS[p]), k_src, v_src)[half]
            cp.start()
            gather[t].setdefault(7, []).append(cp)

    def wait_keys(t, ps):
        for p in ps:
            for cp in gather[t].get(p, []):
                cp.wait_recv()

    for cp in swaps[1]:
        cp.start()
    for cp in own_kv + loads + acc_loads:
        cp.wait()

    c_exp = SCALE * LOG2E
    diff = lax.broadcasted_iota(jnp.int32, (ROWS, CHUNK), 0) - lax.rem(
        lax.broadcasted_iota(jnp.int32, (ROWS, CHUNK), 1), ROWS
    )
    total = 2 * HEADS * ROWS

    def key_group(p):
        return order_ref[lax.rem(chip - OFFSETS[p] + CHIPS, CHIPS) * 2 + core]

    def first_pass(t, a, b):
        keys = kb[t, pl.ds(a * ROWS, (b - a) * ROWS), :]
        values = vb[t, pl.ds(a * ROWS, (b - a) * ROWS), :]

        @pl.loop(0, total // CHUNK, unroll=UNROLL)
        def _(j):
            half = j // (HEADS // 2)
            pair = pl.ds(lax.rem(j, HEADS // 2) * 2, 2)
            qs = qb[t, half, pair].reshape(CHUNK, DIM)
            gs = gb[t, half, pair].reshape(CHUNK, DIM)
            lanes = pl.ds(pl.multiple_of(j * CHUNK, CHUNK), CHUNK)
            s_all = mm(keys, qs, NT)
            d_all = mm(values, gs, NT)
            query_group = order_ref[chip * 2 + half]
            for p in range(a, b):
                part = slice((p - a) * ROWS, (p - a + 1) * ROWS)
                ahead = query_group - key_group(p)
                s = s_all[part]
                if p == 0:
                    s = jnp.where(diff <= ahead * ROWS, s, NEG)
                m = jnp.max(s, axis=0, keepdims=True)
                e = jnp.exp2((s - m) * c_exp)
                d = d_all[part]
                eb[t, pl.ds(p * ROWS, ROWS), lanes] = e
                db[t, pl.ds(p * ROWS, ROWS), lanes] = d
                if p > 0:
                    m = jnp.where(ahead > 0, m, NEG)
                mst[t, pl.ds(p, 1), lanes] = m
                lst[t, pl.ds(p, 1), lanes] = jnp.sum(e, axis=0, keepdims=True)
                dsum[t, pl.ds(p, 1), lanes] = jnp.sum(e * d, axis=0, keepdims=True)

    def stats(t, meanwhile):
        m_b = mst[t]
        m_own = jnp.max(m_b, axis=0, keepdims=True)
        w = jnp.exp2((m_b - m_own) * c_exp)
        l_own = jnp.sum(lst[t] * w, axis=0, keepdims=True)
        d_own = jnp.sum(dsum[t] * w, axis=0, keepdims=True)
        row = lax.broadcasted_iota(jnp.int32, (8, total), 0)
        st_out[t] = jnp.where(row == 0, m_own, jnp.where(row == 1, l_own, d_own))
        cp = remote(st_out.at[t], st_in.at[t], sts.at[t], stv.at[t], partner)
        cp.start()
        meanwhile()
        cp.wait()
        m_far = st_in[t, 0:1, :]
        m = jnp.maximum(m_own, m_far)
        w_own = jnp.exp2((m_own - m) * c_exp)
        w_far = jnp.exp2((m_far - m) * c_exp)
        inv = 1.0 / (l_own * w_own + st_in[t, 1:2, :] * w_far)
        delta = (d_own * w_own + st_in[t, 2:3, :] * w_far) * inv
        fst[0] = jnp.exp2((m_b - m) * c_exp) * inv
        fst[1] = jnp.broadcast_to(delta, (CHIPS, total))

    def second_pass(t, a, b):
        m_rows = (b - a) * ROWS
        acc[...] = jnp.zeros_like(acc)

        @pl.loop(0, total // WIDE, unroll=UNROLL2)
        def _(j):
            lanes = pl.ds(pl.multiple_of(j * WIDE, WIDE), WIDE)
            half = j // (HEADS // 4)
            group = pl.ds(lax.rem(j, HEADS // 4) * 4, 4)
            delta = fst[1, 0:1, lanes]
            for p in range(a, b):
                prob = eb[t, pl.ds(p * ROWS, ROWS), lanes] * fst[0, p : p + 1, lanes]
                ds = prob * (db[t, pl.ds(p * ROWS, ROWS), lanes] - delta)
                pbuf[pl.ds((p - a) * ROWS, ROWS), :] = prob.astype(jnp.bfloat16)
                sbuf[pl.ds(p * ROWS, ROWS), lanes] = ds.astype(jnp.bfloat16)
            pr = pbuf[pl.ds(0, m_rows), :]
            sg = sbuf[pl.ds(a * ROWS, m_rows), lanes]
            acc[0, pl.ds(0, m_rows), :] += mm(sg, qb[t, half, group].reshape(WIDE, DIM))
            acc[1, pl.ds(0, m_rows), :] += mm(pr, gb[t, half, group].reshape(WIDE, DIM))

    def query_terms(t):
        @pl.loop(0, total // WIDE, unroll=UNROLL2)
        def _(j):
            lanes = pl.ds(pl.multiple_of(j * WIDE, WIDE), WIDE)
            dqt[t, :, lanes] = mm(kt[t], sbuf[:, lanes])

        dq_copies[t].start()

    sends = [[], []]
    middle = [[], []]

    def push(t, src, buf, slot, sem_slot, dev, keep):
        cp = remote(src, buf.at[slot], rss.at[t, sem_slot], rsr.at[t, sem_slot], dev)
        cp.start()
        keep.append(cp)

    def send_terms(t, a, b):
        for p in range(a, b):
            rows = pl.ds((p - a) * ROWS, ROWS)
            dk = acc[0, rows, :] * SCALE
            dv = acc[1, rows, :]
            if p == 0:
                acc_own[t, 0] = dk
                acc_own[t, 1] = dv
            elif p in (3, 4):
                mid_own[p - 3, 0] = dk
                mid_own[p - 3, 1] = dv
            else:
                rs_out[t, p, 0] = dk.astype(jnp.bfloat16)
                rs_out[t, p, 1] = dv.astype(jnp.bfloat16)
                if p < 3:
                    push(t, rs_out.at[t, p], rs_in, (t, p), p, peer(sec, -OFFSETS[p]), sends[t])
                elif p < 7:
                    near = p - 4
                    push(t, rs_out.at[t, p], rs_mid, (t, p - 5), p, peer(sec, -OFFSETS[near]), middle[t])
                else:
                    push(t, rs_out.at[t, p, 0], rs_far, (t, 0), 7, peer(sec, -2), middle[t])
                    push(t, rs_out.at[t, p, 1], rs_far, (t, 1), 0, peer(sec, 2), middle[t])

    def relay_terms(t):
        for cp in middle[t]:
            cp.wait_recv()
        for p in (3, 4):
            n = p - 3
            dk = mid_own[n, 0] + rs_mid[t, n, 0].astype(jnp.float32)
            dv = mid_own[n, 1] + rs_mid[t, n, 1].astype(jnp.float32)
            far = rs_far[t, n].astype(jnp.float32)
            if n == 0:
                dk = dk + far
            else:
                dv = dv + far
            rs_out[t, p, 0] = dk.astype(jnp.bfloat16)
            rs_out[t, p, 1] = dv.astype(jnp.bfloat16)
            push(t, rs_out.at[t, p], rs_in, (t, p), p, peer(sec, -OFFSETS[p]), sends[t])

    far_rows = pl.ds(pl.multiple_of((1 - core) * HEADS * ROWS, HEADS * ROWS), HEADS * ROWS)
    dq_copies = [
        remote(dqt.at[t, :, far_rows], dq_in.at[t], dqs.at[t], dqr.at[t], partner) for t in range(2)
    ]

    def finish_queries(t):
        dq_copies[t].wait()
        for h in range(HEADS):
            own = pl.ds(pl.multiple_of(core * HEADS * ROWS + h * ROWS, ROWS), ROWS)
            full = (dqt[t, :, own] + dq_in[t, :, pl.ds(h * ROWS, ROWS)]) * SCALE
            dq_ref[t, 0, :, pl.ds(h * DIM, DIM)] = full.T.astype(jnp.bfloat16)

    def finish_terms(t):
        for cp in sends[t]:
            cp.wait_recv()
        for i in range(2):
            s = acc_own[t, i]
            for p in range(1, 5):
                s = s + rs_in[t, p, i].astype(jnp.float32)
            if t == 0:
                s = s + acc_in[0, i]
            acc_own[t, i] = s

    carry = remote(acc_own.at[0], acc_in.at[1], cs.at[0], cr.at[0], (prev, cx))
    def make_transposed(t, ps):
        for p in ps:
            rows = pl.ds(p * ROWS, ROWS)
            kt[t, :, rows] = kb[t, rows, :].astype(jnp.float32).T.astype(jnp.bfloat16)

    def swap_wait(t):
        for cp in swaps[t]:
            cp.wait_recv()

    def all_second(t):
        for a, b in TERMS[t]:
            second_pass(t, a, b)
            send_terms(t, a, b)

    def ahead():
        make_transposed(0, (5, 6, 7))
        relay_gather(1)
        first_pass(1, 3, 5)

    def between():
        relay_terms(0)
        query_terms(0)
        make_transposed(1, range(3, CHIPS))

    swap_wait(0)
    first_pass(0, 0, 1)
    make_transposed(0, (0,))
    for cp in gather[1][0]:
        cp.wait_recv()
    start_next_gather((1, 2))
    relay_gather(0)
    start_next_gather((3, 4))
    swap_wait(1)
    first_pass(1, 0, 1)
    make_transposed(1, (0,))
    wait_keys(0, (1, 2))
    first_pass(0, 1, 5)
    make_transposed(0, (1, 2, 3, 4))
    wait_keys(1, (1, 2))
    first_pass(1, 1, 3)
    make_transposed(1, (1, 2))
    wait_keys(0, (5, 6, 7))
    first_pass(0, 5, 8)
    stats(0, ahead)
    all_second(0)
    wait_keys(1, (5, 6, 7))
    first_pass(1, 5, 8)
    stats(1, between)
    all_second(1)
    finish_terms(0)
    dk_ref[0, 0] = acc_own[0, 0]
    dv_ref[0, 0] = acc_own[0, 1]

    @pl.when(sec > 0)
    def _():
        carry.start()

    query_terms(1)
    relay_terms(1)
    finish_queries(0)
    finish_queries(1)
    finish_terms(1)

    @pl.when(sec < sections - 1)
    def _():
        carry.wait_recv()
        acc_own[1] = acc_own[1] + acc_in[1]

    dk_ref[1, 0] = acc_own[1, 0]
    dv_ref[1, 0] = acc_own[1, 1]

    @pl.when(sec > 0)
    def _():
        carry.wait_send()

    for t in range(2):
        for cps in gather[t].values():
            for cp in cps:
                cp.wait_send()
        for cp in swaps[t] + middle[t] + sends[t]:
            cp.wait_send()


def body(queries, out_grad, keys, values, entering_keys, entering_values, key_grads_in, value_grads_in, group_order, *, sections):
    arrays = (group_order, queries, out_grad, keys, values, entering_keys, entering_values, key_grads_in, value_grads_in)
    any_spec = pl.BlockSpec(memory_space=pltpu.HBM)
    vmem = pl.BlockSpec(memory_space=pltpu.VMEM)
    total = 2 * HEADS * ROWS
    bf16, f32 = jnp.bfloat16, jnp.float32
    dma = pltpu.SemaphoreType.DMA
    return pl.pallas_call(
        functools.partial(kernel, sections),
        out_shape=(
            jax.ShapeDtypeStruct((2, 1, ROWS, HEADS * DIM), bf16),
            jax.ShapeDtypeStruct((2, 1, ROWS, DIM), f32),
            jax.ShapeDtypeStruct((2, 1, ROWS, DIM), f32),
        ),
        in_specs=[pl.BlockSpec(memory_space=pltpu.SMEM)] + [any_spec] * 8,
        out_specs=(vmem, vmem, vmem),
        scratch_shapes=[
            pltpu.VMEM((2, 2, HEADS, ROWS, DIM), bf16),
            pltpu.VMEM((2, 2, HEADS, ROWS, DIM), bf16),
            pltpu.VMEM((2, CHIPS * ROWS, DIM), bf16),
            pltpu.VMEM((2, CHIPS * ROWS, DIM), bf16),
            pltpu.VMEM((2, DIM, CHIPS * ROWS), bf16),
            pltpu.VMEM((2, CHIPS * ROWS, total), f32),
            pltpu.VMEM((2, CHIPS * ROWS, total), f32),
            pltpu.VMEM((2, CHIPS, total), f32),
            pltpu.VMEM((2, CHIPS, total), f32),
            pltpu.VMEM((2, CHIPS, total), f32),
            pltpu.VMEM((2, CHIPS, total), f32),
            pltpu.VMEM((2, 8, total), f32),
            pltpu.VMEM((2, 8, total), f32),
            pltpu.VMEM((3 * ROWS, WIDE), bf16),
            pltpu.VMEM((CHIPS * ROWS, total), bf16),
            pltpu.VMEM((2, 3 * ROWS, DIM), f32),
            pltpu.VMEM((2, DIM, total), f32),
            pltpu.VMEM((2, DIM, total // 2), f32),
            pltpu.VMEM((2, CHIPS, 2, ROWS, DIM), bf16),
            pltpu.VMEM((2, 5, 2, ROWS, DIM), bf16),
            pltpu.VMEM((2, 2, 2, ROWS, DIM), bf16),
            pltpu.VMEM((2, 2, ROWS, DIM), bf16),
            pltpu.VMEM((2, 2, ROWS, DIM), f32),
            pltpu.VMEM((2, 2, ROWS, DIM), f32),
            pltpu.VMEM((2, 2, ROWS, DIM), f32),
            dma((2, 2, HEADS)),
            dma((2,)),
            dma((2, 2, HEADS)),
            dma((2, 2, HEADS)),
            dma((2, CHIPS, 2)),
            dma((2, CHIPS, 2)),
            dma((2,)),
            dma((2,)),
            dma((2,)),
            dma((2,)),
            dma((2, CHIPS)),
            dma((2, CHIPS)),
            dma((1,)),
            dma((1,)),
            dma((2,)),
        ],
        compiler_params=pltpu.CompilerParams(
            collective_id=0, has_side_effects=True, vmem_limit_bytes=49 << 20
        ),
    )(*(pltpu.with_memory_space_constraint(x, pltpu.HBM) for x in arrays))


def solution(mesh):
    sections = mesh.shape["section"]
    return jax.shard_map(
        functools.partial(body, sections=sections),
        mesh=mesh,
        in_specs=(
            P(None, "section", "ctx", None),
            P(None, "section", "ctx", None),
            P("section", "ctx", None),
            P("section", "ctx", None),
            P("ctx", None),
            P("ctx", None),
            P("section", "ctx", None),
            P("section", "ctx", None),
            P(),
        ),
        out_specs=(
            P(None, "section", "ctx", None),
            P(None, "section", "ctx", None),
            P(None, "section", "ctx", None),
        ),
        check_vma=False,
    )
```

```python
import functools
import math

import jax
import jax.numpy as jnp
from jax import lax
from jax.experimental import pallas as pl
from jax.experimental.pallas import tpu as pltpu
from jax.sharding import PartitionSpec as P

HEADS = 8
DIM = 128
ROWS = 128
CHUNK = 256
WIDE = 512
UNROLL = 4
UNROLL2 = 4
NEG = -1e30
MESH = pl.DeviceIdType.MESH
SCALE = 1.0 / math.sqrt(DIM)
LOG2E = 1.4426950408889634
NT = (((1,), (1,)), ((), ()))
NN = (((1,), (0,)), ((), ()))


def mm(a, b, dims=NN):
    return lax.dot_general(a, b, dims, preferred_element_type=jnp.float32)


OFFSETS = (0, 1, -1, 2, -2, 3, -3, 4)
CHIPS = len(OFFSETS)
NEAR = (3, 4, 1, 2)
TERMS = (((5, 8), (0, 3), (3, 5)), ((7, 8), (5, 7), (0, 3), (3, 5)))


def kernel(
    sections,
    order_ref,
    q_ref,
    g_ref,
    k_ref,
    v_ref,
    ek_ref,
    ev_ref,
    ka_ref,
    va_ref,
    dq_ref,
    dk_ref,
    dv_ref,
    qb,
    gb,
    kb,
    vb,
    kt,
    eb,
    db,
    mst,
    lst,
    dsum,
    fst,
    st_out,
    st_in,
    pbuf,
    sbuf,
    acc,
    dqt,
    dq_in,
    rs_out,
    rs_in,
    rs_mid,
    rs_far,
    mid_own,
    acc_own,
    acc_in,
    load_sem,
    kv_sem,
    xs,
    xr,
    ags,
    agr,
    sts,
    stv,
    dqs,
    dqr,
    rss,
    rsr,
    cs,
    cr,
    acc_sem,
):
    sec = lax.axis_index("section")
    cx = lax.axis_index("ctx")
    chip = cx // 2
    core = lax.rem(cx, 2)
    prev = lax.rem(sec + sections - 1, sections)
    nxt = lax.rem(sec + 1, sections)
    partner = (sec, chip * 2 + 1 - core)

    def peer(section, offset):
        return (section, lax.rem(chip + offset + CHIPS, CHIPS) * 2 + core)

    barrier = pltpu.get_barrier_semaphore()
    for p in range(1, 5):
        pl.semaphore_signal(barrier, inc=1, device_id=peer(sec, OFFSETS[p]), device_id_type=MESH)
    pl.semaphore_signal(barrier, inc=1, device_id=partner, device_id_type=MESH)
    pl.semaphore_signal(barrier, inc=1, device_id=(nxt, cx), device_id_type=MESH)
    pl.semaphore_signal(barrier, inc=1, device_id=(prev, cx), device_id_type=MESH)

    def local(src, dst, sem):
        return pltpu.make_async_copy(src, dst, sem)

    def remote(src, dst, s, r, dev):
        return pltpu.make_async_remote_copy(
            src_ref=src, dst_ref=dst, send_sem=s, recv_sem=r, device_id=dev, device_id_type=MESH
        )

    own_kv = [
        local(k_ref.at[0], kb.at[0, pl.ds(0, ROWS)], kv_sem.at[0]),
        local(v_ref.at[0], vb.at[0, pl.ds(0, ROWS)], kv_sem.at[1]),
    ]
    loads = []
    for t in range(2):
        for i, (src, dst) in enumerate(((q_ref, qb), (g_ref, gb))):
            for h in range(HEADS):
                loads.append(
                    local(
                        src.at[t, 0, :, pl.ds(h * DIM, DIM)],
                        dst.at[t, core, h],
                        load_sem.at[t, i, h],
                    )
                )
    acc_loads = [
        local(ka_ref.at[0], acc_in.at[0, 0], acc_sem.at[0]),
        local(va_ref.at[0], acc_in.at[0, 1], acc_sem.at[1]),
    ]
    for cp in own_kv + loads + acc_loads:
        cp.start()

    pl.semaphore_wait(barrier, 7)

    def kv_copies(t, p, dev, k_src, v_src):
        rows = pl.ds(p * ROWS, ROWS)
        return [
            remote(k_src, kb.at[t, rows], ags.at[t, p, 0], agr.at[t, p, 0], dev),
            remote(v_src, vb.at[t, rows], ags.at[t, p, 1], agr.at[t, p, 1], dev),
        ]

    gather = [{}, {}]
    for p in NEAR:
        gather[0][p] = kv_copies(0, p, peer(sec, OFFSETS[p]), k_ref.at[0], v_ref.at[0])
        for cp in gather[0][p]:
            cp.start()

    swaps = [[], []]
    for t in range(2):
        for i, (src, dst) in enumerate(((q_ref, qb), (g_ref, gb))):
            for h in range(HEADS):
                swaps[t].append(
                    remote(
                        src.at[t, 0, :, pl.ds(h * DIM, DIM)],
                        dst.at[t, core, h],
                        xs.at[t, i, h],
                        xr.at[t, i, h],
                        partner,
                    )
                )
    for cp in swaps[0]:
        cp.start()

    def shift_keys(k_src, v_src):
        return kv_copies(1, 0, (prev, cx), k_src, v_src)

    @pl.when(sec > 0)
    def _():
        for cp in shift_keys(k_ref.at[0], v_ref.at[0]):
            cp.start()

    @pl.when(sec == 0)
    def _():
        for cp in shift_keys(ek_ref, ev_ref):
            cp.start()

    gather[1][0] = shift_keys(k_ref.at[0], v_ref.at[0])

    def start_next_gather(ps):
        rows = pl.ds(0, ROWS)
        for p in ps:
            gather[1][p] = kv_copies(1, p, peer(sec, OFFSETS[p]), kb.at[1, rows], vb.at[1, rows])
            for cp in gather[1][p]:
                cp.start()

    def relay_gather(t):
        gather[t][7] = []
        for i in range(2):
            for p, near, far in ((3, 1, 5), (4, 2, 6)):
                gather[t][p][i].wait_recv()
                rows = pl.ds(p * ROWS, ROWS)
                k_src, v_src = kb.at[t, rows], vb.at[t, rows]
                cp = kv_copies(t, far, peer(sec, OFFSETS[near]), k_src, v_src)[i]
                cp.start()
                gather[t].setdefault(far, []).append(cp)
                if i == p - 3:
                    cp = kv_copies(t, 7, peer(sec, OFFSETS[p]), k_src, v_src)[i]
                    cp.start()
                    gather[t][7].append(cp)

    def wait_keys(t, ps):
        for p in ps:
            for cp in gather[t].get(p, []):
                cp.wait_recv()

    for cp in swaps[1]:
        cp.start()
    for cp in own_kv + loads + acc_loads:
        cp.wait()

    c_exp = SCALE * LOG2E
    diff = lax.broadcasted_iota(jnp.int32, (ROWS, CHUNK), 0) - lax.rem(
        lax.broadcasted_iota(jnp.int32, (ROWS, CHUNK), 1), ROWS
    )
    total = 2 * HEADS * ROWS

    def key_group(p):
        return order_ref[lax.rem(chip - OFFSETS[p] + CHIPS, CHIPS) * 2 + core]

    def first_pass(t, a, b):
        keys = kb[t, pl.ds(a * ROWS, (b - a) * ROWS), :]
        values = vb[t, pl.ds(a * ROWS, (b - a) * ROWS), :]

        @pl.loop(0, total // CHUNK, unroll=UNROLL)
        def _(j):
            half = j // (HEADS // 2)
            pair = pl.ds(lax.rem(j, HEADS // 2) * 2, 2)
            qs = qb[t, half, pair].reshape(CHUNK, DIM)
            gs = gb[t, half, pair].reshape(CHUNK, DIM)
            lanes = pl.ds(pl.multiple_of(j * CHUNK, CHUNK), CHUNK)
            s_all = mm(keys, qs, NT)
            d_all = mm(values, gs, NT)
            query_group = order_ref[chip * 2 + half]
            for p in range(a, b):
                part = slice((p - a) * ROWS, (p - a + 1) * ROWS)
                ahead = query_group - key_group(p)
                s = s_all[part]
                if p == 0:
                    s = jnp.where(diff <= ahead * ROWS, s, NEG)
                m = jnp.max(s, axis=0, keepdims=True)
                e = jnp.exp2((s - m) * c_exp)
                d = d_all[part]
                eb[t, pl.ds(p * ROWS, ROWS), lanes] = e
                db[t, pl.ds(p * ROWS, ROWS), lanes] = d
                if p > 0:
                    m = jnp.where(ahead > 0, m, NEG)
                mst[t, pl.ds(p, 1), lanes] = m
                lst[t, pl.ds(p, 1), lanes] = jnp.sum(e, axis=0, keepdims=True)
                dsum[t, pl.ds(p, 1), lanes] = jnp.sum(e * d, axis=0, keepdims=True)

    def stats(t, meanwhile):
        m_b = mst[t]
        m_own = jnp.max(m_b, axis=0, keepdims=True)
        w = jnp.exp2((m_b - m_own) * c_exp)
        l_own = jnp.sum(lst[t] * w, axis=0, keepdims=True)
        d_own = jnp.sum(dsum[t] * w, axis=0, keepdims=True)
        row = lax.broadcasted_iota(jnp.int32, (8, total), 0)
        st_out[t] = jnp.where(row == 0, m_own, jnp.where(row == 1, l_own, d_own))
        cp = remote(st_out.at[t], st_in.at[t], sts.at[t], stv.at[t], partner)
        cp.start()
        meanwhile()
        cp.wait()
        m_far = st_in[t, 0:1, :]
        m = jnp.maximum(m_own, m_far)
        w_own = jnp.exp2((m_own - m) * c_exp)
        w_far = jnp.exp2((m_far - m) * c_exp)
        inv = 1.0 / (l_own * w_own + st_in[t, 1:2, :] * w_far)
        delta = (d_own * w_own + st_in[t, 2:3, :] * w_far) * inv
        fst[0] = jnp.exp2((m_b - m) * c_exp) * inv
        fst[1] = jnp.broadcast_to(delta, (CHIPS, total))

    def second_pass(t, a, b):
        m_rows = (b - a) * ROWS
        acc[...] = jnp.zeros_like(acc)

        @pl.loop(0, total // WIDE, unroll=UNROLL2)
        def _(j):
            lanes = pl.ds(pl.multiple_of(j * WIDE, WIDE), WIDE)
            half = j // (HEADS // 4)
            group = pl.ds(lax.rem(j, HEADS // 4) * 4, 4)
            delta = fst[1, 0:1, lanes]
            for p in range(a, b):
                prob = eb[t, pl.ds(p * ROWS, ROWS), lanes] * fst[0, p : p + 1, lanes]
                ds = prob * (db[t, pl.ds(p * ROWS, ROWS), lanes] - delta)
                pbuf[pl.ds((p - a) * ROWS, ROWS), :] = prob.astype(jnp.bfloat16)
                sbuf[pl.ds(p * ROWS, ROWS), lanes] = ds.astype(jnp.bfloat16)
            pr = pbuf[pl.ds(0, m_rows), :]
            sg = sbuf[pl.ds(a * ROWS, m_rows), lanes]
            acc[0, pl.ds(0, m_rows), :] += mm(sg, qb[t, half, group].reshape(WIDE, DIM))
            acc[1, pl.ds(0, m_rows), :] += mm(pr, gb[t, half, group].reshape(WIDE, DIM))

    def query_terms(t):
        @pl.loop(0, total // WIDE, unroll=UNROLL2)
        def _(j):
            lanes = pl.ds(pl.multiple_of(j * WIDE, WIDE), WIDE)
            dqt[t, :, lanes] = mm(kt[t], sbuf[:, lanes])

        dq_copies[t].start()

    sends = [{}, {}]
    middle = [{}, {}]

    def push(t, src, buf, slot, sem_slot, dev, keep):
        cp = remote(src, buf.at[slot], rss.at[t, sem_slot], rsr.at[t, sem_slot], dev)
        cp.start()
        keep[sem_slot] = cp

    def send_terms(t, a, b):
        for p in range(a, b):
            rows = pl.ds((p - a) * ROWS, ROWS)
            dk = acc[0, rows, :] * SCALE
            dv = acc[1, rows, :]
            if p == 0:
                acc_own[t, 0] = dk
                acc_own[t, 1] = dv
            elif p in (3, 4):
                mid_own[p - 3, 0] = dk
                mid_own[p - 3, 1] = dv
            else:
                rs_out[t, p, 0] = dk.astype(jnp.bfloat16)
                rs_out[t, p, 1] = dv.astype(jnp.bfloat16)
                if p < 3:
                    push(t, rs_out.at[t, p], rs_in, (t, p), p, peer(sec, -OFFSETS[p]), sends[t])
                elif p < 7:
                    near = p - 4
                    push(t, rs_out.at[t, p], rs_mid, (t, p - 5), p, peer(sec, -OFFSETS[near]), middle[t])
                else:
                    push(t, rs_out.at[t, p, 0], rs_far, (t, 0), 7, peer(sec, -2), middle[t])
                    push(t, rs_out.at[t, p, 1], rs_far, (t, 1), 0, peer(sec, 2), middle[t])

    def relay_terms(t):
        for p in (3, 4):
            n = p - 3
            for slot in ((5, 7), (6, 0))[n]:
                middle[t][slot].wait_recv()
            dk = mid_own[n, 0] + rs_mid[t, n, 0].astype(jnp.float32)
            dv = mid_own[n, 1] + rs_mid[t, n, 1].astype(jnp.float32)
            far = rs_far[t, n].astype(jnp.float32)
            if n == 0:
                dk = dk + far
            else:
                dv = dv + far
            rs_out[t, p, 0] = dk.astype(jnp.bfloat16)
            rs_out[t, p, 1] = dv.astype(jnp.bfloat16)
            push(t, rs_out.at[t, p], rs_in, (t, p), p, peer(sec, -OFFSETS[p]), sends[t])

    far_rows = pl.ds(pl.multiple_of((1 - core) * HEADS * ROWS, HEADS * ROWS), HEADS * ROWS)
    dq_copies = [
        remote(dqt.at[t, :, far_rows], dq_in.at[t], dqs.at[t], dqr.at[t], partner) for t in range(2)
    ]

    def finish_queries(t):
        dq_copies[t].wait()
        for h in range(HEADS):
            own = pl.ds(pl.multiple_of(core * HEADS * ROWS + h * ROWS, ROWS), ROWS)
            full = (dqt[t, :, own] + dq_in[t, :, pl.ds(h * ROWS, ROWS)]) * SCALE
            dq_ref[t, 0, :, pl.ds(h * DIM, DIM)] = full.T.astype(jnp.bfloat16)

    def finish_terms(t):
        for cp in sends[t].values():
            cp.wait_recv()
        for i in range(2):
            s = acc_own[t, i]
            for p in range(1, 5):
                s = s + rs_in[t, p, i].astype(jnp.float32)
            if t == 0:
                s = s + acc_in[0, i]
            acc_own[t, i] = s

    carry = remote(acc_own.at[0], acc_in.at[1], cs.at[0], cr.at[0], (prev, cx))
    def make_transposed(t, ps):
        for p in ps:
            rows = pl.ds(p * ROWS, ROWS)
            kt[t, :, rows] = kb[t, rows, :].astype(jnp.float32).T.astype(jnp.bfloat16)

    def swap_wait(t):
        for cp in swaps[t]:
            cp.wait_recv()

    def all_second(t):
        for a, b in TERMS[t]:
            second_pass(t, a, b)
            send_terms(t, a, b)

    def ahead():
        make_transposed(0, (5, 6, 7))
        relay_gather(1)
        wait_keys(1, (1, 2))
        first_pass(1, 1, 5)

    def between():
        relay_terms(0)
        query_terms(0)
        make_transposed(1, range(1, CHIPS))

    swap_wait(0)
    first_pass(0, 0, 1)
    make_transposed(0, (0,))
    relay_gather(0)
    for cp in gather[1][0]:
        cp.wait_recv()
    start_next_gather((3, 4, 1, 2))
    swap_wait(1)
    first_pass(1, 0, 1)
    make_transposed(1, (0,))
    wait_keys(0, (1, 2))
    first_pass(0, 1, 5)
    make_transposed(0, (1, 2, 3, 4))
    wait_keys(0, (5, 6, 7))
    first_pass(0, 5, 8)
    stats(0, ahead)
    all_second(0)
    wait_keys(1, (5, 6, 7))
    first_pass(1, 5, 8)
    stats(1, between)
    all_second(1)
    finish_terms(0)
    dk_ref[0, 0] = acc_own[0, 0]
    dv_ref[0, 0] = acc_own[0, 1]

    @pl.when(sec > 0)
    def _():
        carry.start()

    query_terms(1)
    finish_queries(0)
    relay_terms(1)
    finish_queries(1)
    finish_terms(1)

    @pl.when(sec < sections - 1)
    def _():
        carry.wait_recv()
        acc_own[1] = acc_own[1] + acc_in[1]

    dk_ref[1, 0] = acc_own[1, 0]
    dv_ref[1, 0] = acc_own[1, 1]

    @pl.when(sec > 0)
    def _():
        carry.wait_send()

    for t in range(2):
        for cps in gather[t].values():
            for cp in cps:
                cp.wait_send()
        for cp in swaps[t] + list(middle[t].values()) + list(sends[t].values()):
            cp.wait_send()


def store_results(a, b, c, out_a, out_b, out_c, sems):
    copies = [
        pltpu.make_async_copy(src, dst, sems.at[i])
        for i, (src, dst) in enumerate(((a, out_a), (b, out_b), (c, out_c)))
    ]
    for cp in copies:
        cp.start()
    for cp in copies:
        cp.wait()


def body(queries, out_grad, keys, values, entering_keys, entering_values, key_grads_in, value_grads_in, group_order, *, sections):
    arrays = (group_order, queries, out_grad, keys, values, entering_keys, entering_values, key_grads_in, value_grads_in)
    any_spec = pl.BlockSpec(memory_space=pltpu.HBM)
    vmem = pl.BlockSpec(memory_space=pltpu.VMEM)
    total = 2 * HEADS * ROWS
    bf16, f32 = jnp.bfloat16, jnp.float32
    dma = pltpu.SemaphoreType.DMA
    results = pl.pallas_call(
        functools.partial(kernel, sections),
        out_shape=(
            jax.ShapeDtypeStruct((2, 1, ROWS, HEADS * DIM), bf16),
            jax.ShapeDtypeStruct((2, 1, ROWS, DIM), f32),
            jax.ShapeDtypeStruct((2, 1, ROWS, DIM), f32),
        ),
        in_specs=[pl.BlockSpec(memory_space=pltpu.SMEM)] + [any_spec] * 8,
        out_specs=(vmem, vmem, vmem),
        scratch_shapes=[
            pltpu.VMEM((2, 2, HEADS, ROWS, DIM), bf16),
            pltpu.VMEM((2, 2, HEADS, ROWS, DIM), bf16),
            pltpu.VMEM((2, CHIPS * ROWS, DIM), bf16),
            pltpu.VMEM((2, CHIPS * ROWS, DIM), bf16),
            pltpu.VMEM((2, DIM, CHIPS * ROWS), bf16),
            pltpu.VMEM((2, CHIPS * ROWS, total), f32),
            pltpu.VMEM((2, CHIPS * ROWS, total), f32),
            pltpu.VMEM((2, CHIPS, total), f32),
            pltpu.VMEM((2, CHIPS, total), f32),
            pltpu.VMEM((2, CHIPS, total), f32),
            pltpu.VMEM((2, CHIPS, total), f32),
            pltpu.VMEM((2, 8, total), f32),
            pltpu.VMEM((2, 8, total), f32),
            pltpu.VMEM((3 * ROWS, WIDE), bf16),
            pltpu.VMEM((CHIPS * ROWS, total), bf16),
            pltpu.VMEM((2, 3 * ROWS, DIM), f32),
            pltpu.VMEM((2, DIM, total), f32),
            pltpu.VMEM((2, DIM, total // 2), f32),
            pltpu.VMEM((2, CHIPS, 2, ROWS, DIM), bf16),
            pltpu.VMEM((2, 5, 2, ROWS, DIM), bf16),
            pltpu.VMEM((2, 2, 2, ROWS, DIM), bf16),
            pltpu.VMEM((2, 2, ROWS, DIM), bf16),
            pltpu.VMEM((2, 2, ROWS, DIM), f32),
            pltpu.VMEM((2, 2, ROWS, DIM), f32),
            pltpu.VMEM((2, 2, ROWS, DIM), f32),
            dma((2, 2, HEADS)),
            dma((2,)),
            dma((2, 2, HEADS)),
            dma((2, 2, HEADS)),
            dma((2, CHIPS, 2)),
            dma((2, CHIPS, 2)),
            dma((2,)),
            dma((2,)),
            dma((2,)),
            dma((2,)),
            dma((2, CHIPS)),
            dma((2, CHIPS)),
            dma((1,)),
            dma((1,)),
            dma((2,)),
        ],
        compiler_params=pltpu.CompilerParams(
            collective_id=0, has_side_effects=True, vmem_limit_bytes=49 << 20
        ),
    )(*(pltpu.with_memory_space_constraint(x, pltpu.HBM) for x in arrays))
    return pl.pallas_call(
        store_results,
        out_shape=tuple(jax.ShapeDtypeStruct(r.shape, r.dtype) for r in results),
        in_specs=[pl.BlockSpec(memory_space=pltpu.VMEM)] * 3,
        out_specs=(pl.BlockSpec(memory_space=pl.ANY),) * 3,
        scratch_shapes=[dma((3,))],
        compiler_params=pltpu.CompilerParams(vmem_limit_bytes=4 << 20),
    )(*results)


def solution(mesh):
    sections = mesh.shape["section"]
    return jax.shard_map(
        functools.partial(body, sections=sections),
        mesh=mesh,
        in_specs=(
            P(None, "section", "ctx", None),
            P(None, "section", "ctx", None),
            P("section", "ctx", None),
            P("section", "ctx", None),
            P("ctx", None),
            P("ctx", None),
            P("section", "ctx", None),
            P("section", "ctx", None),
            P(),
        ),
        out_specs=(
            P(None, "section", "ctx", None),
            P(None, "section", "ctx", None),
            P(None, "section", "ctx", None),
        ),
        check_vma=False,
    )
```
